32 devices in a mesh: rep: 4 (over x, core), fsdp: 8 (over z, y).
Axes of the slice: x: 2, y: 2, z: 4, core: 2. Of those that a mesh axis runs over, the one named last changes fastest.
Arguments:
- inputs: bfloat16 [32, 512, 1536], P(('rep', 'fsdp')), may hold values from -6 to 6
- cotangent: bfloat16 [32, 512, 1536], P(('rep', 'fsdp')), may hold values from -6 to 6
- lengths: int32 [32], P(('rep', 'fsdp')), may hold values from 128 to 512, as said below
- choices: int32 [32, 512, 8], P(('rep', 'fsdp')), may hold values from 0 to 15, all different within a row
- gain_attn: bfloat16 [1536], P('fsdp'), may hold values from 0.099609375 to 1.8984375
- gain_moe: bfloat16 [1536], P('fsdp'), may hold values from 0.099609375 to 1.8984375
- query_weight: bfloat16 [1536, 1536], P('fsdp'), may hold values from -0.15625 to 0.15625
- key_weight: bfloat16 [1536, 512], P('fsdp'), may hold values from -0.15625 to 0.15625
- value_weight: bfloat16 [1536, 512], P('fsdp'), may hold values from -0.15625 to 0.15625
- w_out: bfloat16 [1536, 1536], P('fsdp'), may hold values from -0.625 to 0.625
- w_router: bfloat16 [1536, 16], P('fsdp'), may hold values from -0.078125 to 0.078125
- w_gate: bfloat16 [16, 1536, 512], P('fsdp'), may hold values from -0.15625 to 0.15625
- w_up: bfloat16 [16, 1536, 512], P('fsdp'), may hold values from -0.15625 to 0.15625
- w_down: bfloat16 [16, 512, 1536], P('fsdp'), may hold values from -0.75 to 0.75
Outputs:
- output: bfloat16 [32, 512, 1536], P(('rep', 'fsdp'))
- grad_input: bfloat16 [32, 512, 1536], P(('rep', 'fsdp'))
- grad_gain_attn: float32 [1536], P('fsdp')
- grad_gain_moe: float32 [1536], P('fsdp')
- grad_query: float32 [1536, 1536], P('fsdp')
- grad_key: float32 [1536, 512], P('fsdp')
- grad_value: float32 [1536, 512], P('fsdp')
- grad_out: float32 [1536, 1536], P('fsdp')
- grad_router: float32 [1536, 16], P('fsdp')
- grad_gate: float32 [16, 1536, 512], P('fsdp')
- grad_up: float32 [16, 1536, 512], P('fsdp')
- grad_down: float32 [16, 512, 1536], P('fsdp')
The draws below stay inside these ranges and needn't reach their ends.
Inputs may be any that keep to these rules, and one draw needn't show every extreme that they name: `lengths`: valid tokens of each sequence of 512 slots, from its start; some sequence is full. `choices`: a token's 8 experts are distinct; those of padding tokens are ignored.
All inputs are finite; a program needn't handle non-finite values.
Results may differ from the reference program's by a relative error of at most 0.023.
Values may be sent and summed in bfloat16 or wider, within the bound.
No kernel may reach another device: no remote copies, remote signals or barrier semaphores. Data moves between devices by JAX's collectives and lax.ppermute only.
A program may use at most 320 MiB of HBM per device.

```python
import math
import jax
import jax.numpy as jnp
from jax import lax

MODEL_WIDTH = 1536
QUERY_HEADS = 24
KEY_VALUE_HEADS = 8
HEAD_SIZE = 64
FF = 512
TOPK = 8
SLOTS = 512
SEQS = 32
EXPERTS = 16
CAP = 200


def draw_lengths(key, part):
    first_key, second_key = jax.random.split(jax.random.fold_in(key, 11))
    spread = jax.random.randint(first_key, (SEQS,), SLOTS // 4, SLOTS + 1, dtype=jnp.int32)
    longest = jax.random.randint(second_key, (), 0, SEQS, dtype=jnp.int32)
    return jnp.where(jnp.arange(SEQS, dtype=jnp.int32) == longest, SLOTS, spread).astype(jnp.int32)


def steps_of(key, extent, cuts, smallest, top_value):
    loudness, own = 1.0, jax.random.fold_in(key, 6)
    for dim, shards_of in cuts:
        draws = jnp.exp(jax.random.uniform(jax.random.fold_in(own, dim), (shards_of,), jnp.float32, smallest / len(cuts), top_value / len(cuts)))
        loudness = loudness * jnp.repeat(draws, extent[dim] // shards_of).reshape([-1 if axis == dim else 1 for axis in range(len(extent))])
    return loudness


def distinct(own_key, rows, number_of, top, lift):
    order = jax.random.permutation(jax.random.fold_in(own_key, 1), number_of)
    boost = order
    for power in range(3):
        boost = boost * boost // number_of
    boost = boost * lift // number_of
    tickets = jax.random.randint(jax.random.fold_in(own_key, 2), (rows, number_of), 0, 4096) + boost
    fixed_rows = jax.random.permutation(jax.random.fold_in(own_key, 3), rows)[jnp.arange(number_of) % rows]
    tickets = jnp.where(jnp.arange(rows)[:, None] == fixed_rows[None, :], 1 << 14, tickets)
    priority = tickets * number_of + jnp.arange(number_of)
    return lax.top_k(priority.astype(jnp.int32), top)[1].astype(jnp.int32)


def centred(stream_key, dims, scale, bound, cuts=(), held_as=jnp.bfloat16):
    gain = steps_of(stream_key, dims, cuts, -0.22, 0.18) if cuts else 1.0
    drawn = jax.random.normal(stream_key, dims, jnp.float32) * scale * gain
    return jnp.minimum(jnp.maximum(drawn, -bound), bound).astype(held_as)


def setup_inputs(seed: int = 0) -> dict:
    key_of = jax.random.split(jax.random.key(seed), 15)
    inputs = centred(key_of[0], (SEQS, SLOTS, MODEL_WIDTH), 1.0, 6.0, ((0, 32),))
    cotangent = centred(key_of[1], (SEQS, SLOTS, MODEL_WIDTH), 1.0, 6.0, ((0, 32),))
    lengths = draw_lengths(jax.random.fold_in(key_of[14], 71), 0)
    choices = distinct(key_of[3], SEQS * SLOTS, EXPERTS, TOPK, 4096).reshape((SEQS, SLOTS, TOPK))
    gain_attn = jnp.clip(1.0 + 0.18 * jax.random.normal(key_of[4], (MODEL_WIDTH,), jnp.float32), 0.099609375, 1.8984375).astype(jnp.bfloat16)
    gain_moe = jnp.clip(1.0 + 0.18 * jax.random.normal(key_of[5], (MODEL_WIDTH,), jnp.float32), 0.099609375, 1.8984375).astype(jnp.bfloat16)
    query_weight = centred(key_of[6], (MODEL_WIDTH, QUERY_HEADS * HEAD_SIZE), MODEL_WIDTH ** -0.5, 0.15625, ((0, 8),))
    key_weight = centred(key_of[7], (MODEL_WIDTH, KEY_VALUE_HEADS * HEAD_SIZE), MODEL_WIDTH ** -0.5, 0.15625, ((0, 8),))
    value_weight = centred(key_of[8], (MODEL_WIDTH, KEY_VALUE_HEADS * HEAD_SIZE), MODEL_WIDTH ** -0.5, 0.15625, ((0, 8),))
    w_out = centred(key_of[9], (QUERY_HEADS * HEAD_SIZE, MODEL_WIDTH), (QUERY_HEADS * HEAD_SIZE // 16) ** -0.5, 0.625, ((0, 8),))
    w_router = centred(key_of[10], (MODEL_WIDTH, EXPERTS), (4 * MODEL_WIDTH) ** -0.5, 0.078125, ((0, 8),))
    w_gate = centred(key_of[11], (EXPERTS, MODEL_WIDTH, FF), MODEL_WIDTH ** -0.5, 0.15625, ((0, 8),))
    w_up = centred(key_of[12], (EXPERTS, MODEL_WIDTH, FF), MODEL_WIDTH ** -0.5, 0.15625, ((0, 8),))
    w_down = centred(key_of[13], (EXPERTS, FF, MODEL_WIDTH), (FF // 8) ** -0.5, 0.75, ((0, 8),))
    return dict(inputs=inputs, cotangent=cotangent, lengths=lengths, choices=choices, gain_attn=gain_attn, gain_moe=gain_moe, query_weight=query_weight, key_weight=key_weight, value_weight=value_weight, w_out=w_out, w_router=w_router, w_gate=w_gate, w_up=w_up, w_down=w_down)


@jax.custom_vjp
def lowered_precision(v):
    return lax.optimization_barrier(v.astype(jnp.bfloat16)).astype(jnp.float32)

@jax.custom_vjp
def lowered_backward(v):
    return v

def low_keep(v):
    return (lowered_precision(v), None)

def low_pass(kept, grad):
    return (grad,)

def back_keep(v):
    return (v, None)

def back_low(kept, grad):
    return (lowered_precision(grad),)
lowered_precision.defvjp(low_keep, low_pass)
lowered_backward.defvjp(back_keep, back_low)
HIGHEST = lax.Precision.HIGHEST

def precise_product(left_side, right_side):
    return jnp.dot(left_side, right_side, precision=HIGHEST)

def rms_scale(value_rows, gain_vec):
    inverse = lax.rsqrt(lax.optimization_barrier(jnp.mean(value_rows * value_rows, axis=-1, keepdims=True)) + 1e-05)
    return value_rows * inverse * gain_vec

def rotation(expert_slot_count, head_dim):
    half_dim = head_dim // 2
    frequency = jnp.exp(-jnp.log(10000.0) * 2.0 * jnp.arange(half_dim, dtype=jnp.float32) / head_dim)
    angles = jnp.arange(expert_slot_count, dtype=jnp.float32)[:, None] * frequency[None, :]
    return (jnp.cos(angles), jnp.sin(angles))

def rotary_apply(value_rows, cosine_table, sine_table):
    half_dim = value_rows.shape[-1] // 2
    extra_dims = (1,) * (value_rows.ndim - 2)
    cosine_table = cosine_table.reshape(cosine_table.shape[:1] + extra_dims + cosine_table.shape[1:])
    sine_table = sine_table.reshape(sine_table.shape[:1] + extra_dims + sine_table.shape[1:])
    first_half = value_rows[..., :half_dim]
    second = value_rows[..., half_dim:]
    return jnp.concatenate([first_half * cosine_table - second * sine_table, second * cosine_table + first_half * sine_table], axis=-1)

def route_pairs(choices_row, length, experts, capacity):
    expert_slot_count, top_count = choices_row.shape
    valid_rows = jnp.arange(expert_slot_count, dtype=jnp.int32) < length
    marks_hit = (choices_row[:, :, None] == jnp.arange(experts, dtype=jnp.int32)[None, None, :]) & valid_rows[:, None, None]
    marks_hit = marks_hit.astype(jnp.int32).reshape(expert_slot_count * top_count, experts)
    before = jnp.cumsum(marks_hit, axis=0) - marks_hit
    position = lax.optimization_barrier(jnp.sum(before * marks_hit, axis=1)).reshape(expert_slot_count, top_count)
    kept_pairs = valid_rows[:, None] & (position < capacity)
    slot_index = jnp.where(kept_pairs, choices_row * capacity + position, experts * capacity).astype(jnp.int32)
    token_ids = jnp.repeat(jnp.arange(expert_slot_count, dtype=jnp.int32), top_count)
    source_token = jnp.full((experts * capacity,), expert_slot_count, jnp.int32).at[slot_index.reshape(-1)].set(token_ids, mode='drop')
    return (kept_pairs, slot_index, source_token)

def forward(inputs, gain_attn, gain_moe, query_weight, key_weight, value_weight, w_out, w_router, w_gate, w_up, w_down, length, choices_row):
    expert_slot_count, width = inputs.shape
    query_group_width = QUERY_HEADS // KEY_VALUE_HEADS
    scale_factor = 1.0 / math.sqrt(HEAD_SIZE)
    cosine_table, sine_table = rotation(expert_slot_count, HEAD_SIZE)
    attention_normed = lowered_precision(rms_scale(inputs, gain_attn))
    query_rows = lowered_backward(precise_product(attention_normed, query_weight)).reshape(expert_slot_count, KEY_VALUE_HEADS, query_group_width, HEAD_SIZE)
    unrotated_keys = lowered_backward(precise_product(attention_normed, key_weight)).reshape(expert_slot_count, KEY_VALUE_HEADS, HEAD_SIZE)
    value_rows = lowered_precision(lowered_backward(precise_product(attention_normed, value_weight))).reshape(expert_slot_count, KEY_VALUE_HEADS, HEAD_SIZE)
    rot_queries = lowered_precision(rotary_apply(query_rows, cosine_table, sine_table))
    rot_keys = lowered_precision(rotary_apply(unrotated_keys, cosine_table, sine_table))
    scores = lowered_backward(jnp.einsum('qhgd,khd->hgqk', rot_queries, rot_keys, precision=HIGHEST) * scale_factor)
    rows_index = jnp.arange(expert_slot_count, dtype=jnp.int32)
    allowed = (rows_index[None, :] <= rows_index[:, None]) & (rows_index[None, :] < length)
    scores = jnp.where(allowed, scores, -1e+30)
    probs = jax.nn.softmax(scores, axis=-1)
    mixed = jnp.einsum('hgqk,khd->qhgd', lowered_precision(probs), value_rows, precision=HIGHEST).reshape(expert_slot_count, QUERY_HEADS * HEAD_SIZE)
    mixed = lowered_precision(lowered_backward(mixed))
    hidden = inputs + lowered_backward(precise_product(mixed, w_out))
    normed_two = lowered_precision(rms_scale(hidden, gain_moe))
    logits = lowered_backward(precise_product(normed_two, w_router))
    gates = jax.nn.softmax(jnp.take_along_axis(logits, choices_row, axis=1), axis=-1)
    kept_pairs, slot_index, source_token = route_pairs(choices_row, length, EXPERTS, CAP)
    expert_rows = lowered_backward(jnp.take(normed_two, source_token, axis=0, mode='fill', fill_value=0.0)).reshape(EXPERTS, CAP, width)
    gate_part = lowered_backward(jnp.einsum('ecd,edf->ecf', expert_rows, w_gate, precision=HIGHEST))
    up_part = lowered_backward(jnp.einsum('ecd,edf->ecf', expert_rows, w_up, precision=HIGHEST))
    inner = lowered_precision(jax.nn.silu(gate_part) * up_part)
    expert_out = lowered_precision(lowered_backward(jnp.einsum('ecf,efd->ecd', inner, w_down, precision=HIGHEST))).reshape(EXPERTS * CAP, width)
    picked = jnp.take(expert_out, slot_index, axis=0, mode='fill', fill_value=0.0)
    mixture = lax.optimization_barrier(jnp.sum((gates * kept_pairs)[:, :, None] * picked, axis=1))
    valid_rows = (rows_index < length)[:, None]
    return jnp.where(valid_rows, hidden + mixture, 0.0)

def reference(inputs, cotangent, lengths, choices, gain_attn, gain_moe, query_weight, key_weight, value_weight, w_out, w_router, w_gate, w_up, w_down):
    weights = tuple((weight_arg.astype(jnp.float32) for weight_arg in (gain_attn, gain_moe, query_weight, key_weight, value_weight, w_out, w_router, w_gate, w_up, w_down)))

    def one_sequence(totals, sequence):
        tokens, grad_seq, length, choices_row = sequence

        def apply_layer(layer_in, *params):
            return forward(layer_in, *params, length, choices_row)
        result, pull_back = jax.vjp(apply_layer, tokens.astype(jnp.float32), *weights)
        gradients = pull_back(grad_seq.astype(jnp.float32))
        totals = tuple((running + fresh_grad for running, fresh_grad in zip(totals, gradients[1:])))
        return (totals, (result.astype(jnp.bfloat16), gradients[0].astype(jnp.bfloat16)))
    zero_grads = tuple((jnp.zeros_like(weight_arg) for weight_arg in weights))
    totals, outputs = lax.scan(one_sequence, zero_grads, (inputs, cotangent, lengths, choices))
    return (outputs[0], outputs[1], totals[0], totals[1], totals[2], totals[3], totals[4], totals[5], totals[6], totals[7], totals[8], totals[9])
```

```python
import functools
import math

import jax
import jax.numpy as jnp
from jax import lax
from jax.experimental import pallas as pl
from jax.experimental.pallas import tpu as pltpu
from jax.sharding import PartitionSpec as P

QUERY_HEADS = 24
KEY_VALUE_HEADS = 8
HEAD_SIZE = 64
BF16 = jnp.bfloat16
F32 = jnp.float32
ALL = ("fsdp", "rep")
SMALL = 128


def rms_scale(value_rows, gain_vec):
    inverse = lax.rsqrt(jnp.mean(value_rows * value_rows, axis=-1, keepdims=True) + 1e-05)
    return value_rows * inverse * gain_vec


def rotation(expert_slot_count, head_dim):
    half_dim = head_dim // 2
    frequency = jnp.exp(
        -jnp.log(10000.0) * 2.0 * jnp.arange(half_dim, dtype=jnp.float32) / head_dim
    )
    angles = jnp.arange(expert_slot_count, dtype=jnp.float32)[:, None] * frequency[None, :]
    return (jnp.cos(angles), jnp.sin(angles))


def rotary_apply(value_rows, cosine_table, sine_table):
    half_dim = value_rows.shape[-1] // 2
    extra_dims = (1,) * (value_rows.ndim - 2)
    cosine_table = cosine_table.reshape(
        cosine_table.shape[:1] + extra_dims + cosine_table.shape[1:]
    )
    sine_table = sine_table.reshape(sine_table.shape[:1] + extra_dims + sine_table.shape[1:])
    first_half = value_rows[..., :half_dim]
    second = value_rows[..., half_dim:]
    return jnp.concatenate(
        [
            first_half * cosine_table - second * sine_table,
            second * cosine_table + first_half * sine_table,
        ],
        axis=-1,
    )


def slot_table(choices_row, length, experts, capacity):
    slots = choices_row.shape[0]
    valid = (jnp.arange(slots, dtype=jnp.int32) < length)[:, None]
    chosen = jnp.any(
        choices_row[:, :, None] == jnp.arange(experts, dtype=jnp.int32)[None, None, :], axis=1
    )
    hit = (chosen & valid).astype(F32)
    rows = jnp.arange(slots, dtype=jnp.int32)
    earlier = (rows[None, :] < rows[:, None]).astype(BF16)
    position = jnp.dot(earlier, hit.astype(BF16), preferred_element_type=F32).astype(jnp.int32)
    kept = chosen & valid & (position < capacity)
    return jnp.where(kept, position, jnp.where(chosen, -1, -2))


def chosen_gates(logits, table):
    chosen = table >= -1
    masked = jnp.where(chosen, logits, -1e30)
    top = jnp.max(masked, axis=-1, keepdims=True)
    raised = jnp.where(chosen, jnp.exp(masked - top), 0.0)
    return raised / jnp.sum(raised, axis=-1, keepdims=True)


def ring_order(size):
    if size % 2:
        return list(range(size))
    return list(range(0, size, 2)) + list(range(size - 1, 0, -2))


def shift(value, order, step):
    size = len(order)
    return lax.ppermute(value, "fsdp", [(order[i], order[(i + step) % size]) for i in range(size)])


def ring_gather(value, order):
    size = len(order)
    found = {0: value}
    ahead = back = value
    for step in range(1, (size - 1) // 2 + 1):
        back = shift(back, order, 1)
        ahead = shift(ahead, order, -1)
        found[-step] = back
        found[step] = ahead
    if size % 2 == 0:
        half = value.shape[0] // 2
        top = shift(back[:half], order, 1)
        bottom = shift(ahead[half:], order, -1)
        found[size // 2] = jnp.concatenate([top, bottom], axis=0)
    return found


def add_low(left, right):
    return (left.astype(F32) + right.astype(F32)).astype(BF16)


def ring_scatter(parts, order):
    size = len(order)
    near = (size - 1) // 2
    if size % 2 == 0:
        far = parts[size // 2]
        half = far.shape[0] // 2
        top = shift(far[:half], order, 1)
        bottom = shift(far[half:], order, -1)
        ahead, back = parts[near], parts[-near]
        ahead = jnp.concatenate([add_low(ahead[:half], top), ahead[half:]], axis=0)
        back = jnp.concatenate([back[:half], add_low(back[half:], bottom)], axis=0)
    else:
        ahead, back = parts[near], parts[-near]
    for step in range(near, 0, -1):
        ahead = shift(ahead, order, 1)
        back = shift(back, order, -1)
        if step > 1:
            ahead = add_low(parts[step - 1], ahead)
            back = add_low(parts[1 - step], back)
    return ahead, back


def three_way(value):
    high = value.astype(BF16)
    rest = value - high.astype(F32)
    middle = rest.astype(BF16)
    low = (rest - middle.astype(F32)).astype(BF16)
    return high, middle, low


def dot_nn(left, right):
    return jnp.dot(left, right, preferred_element_type=F32)


def dot_nt(left, right):
    return lax.dot_general(left, right, (((1,), (1,)), ((), ())), preferred_element_type=F32)


def expert_kernel(
    first_ref,
    seq_ref,
    tok_ref,
    cot_ref,
    row_ref,
    col_ref,
    router_ref,
    gate_ref,
    up_ref,
    down_ref,
    *rest,
    padded,
):
    (
        out_ref,
        grad_ref,
        gg_ref,
        rows_ref,
        geo_ref,
        inner_ref,
        ggp_ref,
        gup_ref,
        gates_scr,
        out_acc,
        grad_acc,
    ) = rest[-11:]
    e = pl.program_id(1)
    tok = tok_ref[0]
    cot = cot_ref[0]
    slots = tok.shape[0]
    table = col_ref[0]
    lanes = lax.broadcasted_iota(jnp.int32, table.shape, 1)

    @pl.when(e == 0)
    def _():
        gates_scr[...] = chosen_gates(dot_nn(tok, router_ref[...]), table)
        out_acc[...] = jnp.zeros_like(out_acc)
        grad_acc[...] = jnp.zeros_like(grad_acc)
        gg_ref[0] = jnp.zeros_like(gg_ref[0])

    mine = lanes == first_ref[0] + e
    gate_lane = jnp.where(mine, gates_scr[...], 0.0)
    gate_col = jnp.sum(gate_lane, axis=1, keepdims=True)
    pos_col = jnp.sum(jnp.where(mine, table.astype(F32), 0.0), axis=1, keepdims=True).astype(jnp.int32)
    pos_row = row_ref[0, 0]
    pick = (lax.broadcasted_iota(jnp.int32, (padded, slots), 0) == pos_row).astype(F32).astype(BF16)
    place = (lax.broadcasted_iota(jnp.int32, (slots, padded), 1) == pos_col).astype(F32).astype(BF16)

    rows = dot_nn(pick, tok).astype(BF16)
    cot_rows = dot_nn(pick, cot)
    high, middle, low = three_way(gate_lane)
    gate_slot = dot_nn(pick, high) + dot_nn(pick, middle) + dot_nn(pick, low)
    gate_slot = jnp.sum(gate_slot, axis=1, keepdims=True)
    rows_ref[0, 0] = rows

    gate_part = dot_nn(rows, gate_ref[0])
    up_part = dot_nn(rows, up_ref[0])
    sig = 1.0 / (1.0 + jnp.exp(-gate_part))
    silu = gate_part * sig
    inner = (silu * up_part).astype(BF16)
    inner_ref[0, 0] = inner
    expert_out = dot_nn(inner, down_ref[0]).astype(BF16)
    out_acc[...] += gate_col * dot_nn(place, expert_out)

    dots = jnp.sum(cot_rows * expert_out.astype(F32), axis=1, keepdims=True)
    spread = jnp.where(lax.broadcasted_iota(jnp.int32, (padded, SMALL), 1) == e, dots, 0.0)
    high, middle, low = three_way(spread)
    gg_ref[0] += dot_nn(place, high) + dot_nn(place, middle) + dot_nn(place, low)

    geo = (gate_slot * cot_rows).astype(BF16)
    geo_ref[0, 0] = geo
    grad_inner = dot_nt(geo, down_ref[0])
    ggp = (grad_inner * up_part * sig * (1.0 + gate_part * (1.0 - sig))).astype(BF16)
    gup = (grad_inner * silu).astype(BF16)
    ggp_ref[0, 0] = ggp
    gup_ref[0, 0] = gup
    grad_rows = (dot_nt(ggp, gate_ref[0]) + dot_nt(gup, up_ref[0])).astype(BF16)
    grad_acc[...] += dot_nn(place, grad_rows)

    @pl.when(e == pl.num_programs(1) - 1)
    def _():
        out_ref[0] = out_acc[...].astype(BF16)
        grad_ref[0] = grad_acc[...].astype(BF16)


def run_experts(first, seqs, tok, cot, rows_table, cols_table, router, w_gate, w_up, w_down, padded, kept, start, total):
    count, slots, width = tok.shape
    local, _, ff = w_gate.shape
    row_block = lambda s, e, first, seq: (seq[s], first[0] + e, 0, 0)
    col_block = lambda s, e, first, seq: (seq[s], 0, 0)
    seq_block = lambda s, e, first, seq: (s, 0, 0)
    slot_block = lambda s, e, first, seq: (start + s, e, 0, 0)
    expert_block = lambda s, e, first, seq: (e, 0, 0)
    wide = jax.ShapeDtypeStruct((total, local, padded, width), BF16)
    thin = jax.ShapeDtypeStruct((total, local, padded, ff), BF16)
    whole = jax.ShapeDtypeStruct((count, slots, width), BF16)
    flops = 2 * count * local * (padded * width * (6 * ff + 4 * slots))
    moved = 4 * count * slots * width * 2 + count * local * (3 * width * ff + padded * (2 * width + 3 * ff)) * 2
    return pl.pallas_call(
        functools.partial(expert_kernel, padded=padded),
        out_shape=(
            whole,
            whole,
            jax.ShapeDtypeStruct((count, slots, SMALL), F32),
            wide,
            wide,
            thin,
            thin,
            thin,
        ),
        grid_spec=pltpu.PrefetchScalarGridSpec(
            num_scalar_prefetch=2,
            grid=(count, local),
            in_specs=[
                pl.BlockSpec((1, slots, width), seq_block),
                pl.BlockSpec((1, slots, width), seq_block),
                pl.BlockSpec((1, 1, 1, slots), row_block),
                pl.BlockSpec((1, slots, SMALL), col_block),
                pl.BlockSpec((width, SMALL), lambda s, e, first, seq: (0, 0)),
                pl.BlockSpec((1, width, ff), expert_block),
                pl.BlockSpec((1, width, ff), expert_block),
                pl.BlockSpec((1, ff, width), expert_block),
            ]
            + [pl.BlockSpec(memory_space=pl.ANY)] * len(kept),
            out_specs=[
                pl.BlockSpec((1, slots, width), seq_block),
                pl.BlockSpec((1, slots, width), seq_block),
                pl.BlockSpec((1, slots, SMALL), seq_block),
                pl.BlockSpec((1, 1, padded, width), slot_block),
                pl.BlockSpec((1, 1, padded, width), slot_block),
                pl.BlockSpec((1, 1, padded, ff), slot_block),
                pl.BlockSpec((1, 1, padded, ff), slot_block),
                pl.BlockSpec((1, 1, padded, ff), slot_block),
            ],
            scratch_shapes=[
                pltpu.VMEM((slots, SMALL), F32),
                pltpu.VMEM((slots, width), F32),
                pltpu.VMEM((slots, width), F32),
            ],
        ),
        input_output_aliases={10 + i: 3 + i for i in range(len(kept))},
        compiler_params=pltpu.CompilerParams(
            dimension_semantics=("arbitrary", "arbitrary"), vmem_limit_bytes=58 * 1024 * 1024
        ),
        cost_estimate=pl.CostEstimate(flops=flops, bytes_accessed=moved, transcendentals=count * local * padded * ff),
    )(first, seqs, tok, cot, rows_table, cols_table, router, w_gate, w_up, w_down, *kept)


def body(
    inputs,
    cotangent,
    lengths,
    choices,
    gain_attn,
    gain_moe,
    query_weight,
    key_weight,
    value_weight,
    w_out,
    w_router,
    w_gate,
    w_up,
    w_down,
):
    groups = lax.axis_size("fsdp")
    replicas = lax.axis_size("rep")
    me = lax.axis_index("fsdp")
    rep = lax.axis_index("rep")
    tokens = inputs[0].astype(F32)
    slots, width = tokens.shape
    length = lengths[0]
    choices_row = choices[0]
    top_count = choices_row.shape[1]
    local = w_gate.shape[0]
    experts = local * groups
    capacity = 25 * slots * top_count // (32 * experts)
    padded = -(-capacity // 16) * 16
    group_width = QUERY_HEADS // KEY_VALUE_HEADS
    scale_factor = 1.0 / math.sqrt(HEAD_SIZE)
    q_width = query_weight.shape[1]
    k_width = key_weight.shape[1]
    cosine_table, sine_table = rotation(slots, HEAD_SIZE)
    order = ring_order(groups)
    place_of = [order.index(j) for j in range(groups)]
    my_place = jnp.asarray(place_of, jnp.int32)[me]

    small = jnp.concatenate(
        [
            w_router,
            gain_attn[:, None],
            gain_moe[:, None],
            jnp.zeros((w_router.shape[0], SMALL - experts - 2), BF16),
        ],
        axis=1,
    )
    share = query_weight.shape[0] // replicas

    def gather_weight(shard):
        piece = lax.dynamic_slice_in_dim(shard, rep * share, share, axis=0)
        return lax.all_gather(piece, ALL, axis=0, tiled=True)

    first_set = gather_weight(
        jnp.concatenate([query_weight, key_weight, value_weight, small], axis=1)
    )
    full_qkv = first_set[:, : q_width + 2 * k_width]
    full_small = first_set[:, q_width + 2 * k_width :]
    full_out = gather_weight(w_out)
    full_gain_attn = full_small[:, experts].astype(F32)
    full_gain_moe = full_small[:, experts + 1].astype(F32)
    lane = jnp.arange(SMALL)[None, :]
    full_router = jnp.where(lane < experts, full_small, jnp.zeros_like(full_small))

    table = slot_table(choices_row, length, experts, capacity)
    row_tables = lax.all_gather(table.T, "fsdp", axis=0, tiled=False)
    col_tables = jnp.pad(
        jnp.swapaxes(row_tables, 1, 2), ((0, 0), (0, 0), (0, SMALL - experts)), constant_values=-2
    )
    row_tables = row_tables[:, :, None, :]
    cot_ring = ring_gather(lax.optimization_barrier((cotangent[0], first_set))[0], order)

    normed_float, norm_one_pull = jax.vjp(rms_scale, tokens, full_gain_attn)
    attention_normed = normed_float.astype(BF16)
    query_rows = jnp.dot(
        attention_normed, full_qkv[:, :q_width], preferred_element_type=F32
    ).reshape(slots, KEY_VALUE_HEADS, group_width, HEAD_SIZE)
    unrotated_keys = jnp.dot(
        attention_normed, full_qkv[:, q_width : q_width + k_width], preferred_element_type=F32
    ).reshape(slots, KEY_VALUE_HEADS, HEAD_SIZE)
    value_rows = (
        jnp.dot(attention_normed, full_qkv[:, q_width + k_width :], preferred_element_type=F32)
        .astype(BF16)
        .reshape(slots, KEY_VALUE_HEADS, HEAD_SIZE)
    )
    rot_queries = rotary_apply(query_rows, cosine_table, sine_table).astype(BF16)
    rot_keys = rotary_apply(unrotated_keys, cosine_table, sine_table).astype(BF16)
    rows_index = jnp.arange(slots, dtype=jnp.int32)
    allowed = (rows_index[None, :] <= rows_index[:, None]) & (rows_index[None, :] < length)

    def masked_scores():
        raw_scores = (
            jnp.einsum("qhgd,khd->hgqk", rot_queries, rot_keys, preferred_element_type=F32)
            * scale_factor
        )
        return jnp.where(allowed, raw_scores, -1e30)

    scores = masked_scores()
    log_total = jax.nn.logsumexp(scores, axis=-1, keepdims=True)
    probs_low = jnp.exp(scores - log_total).astype(BF16)
    mixed = jnp.einsum("hgqk,khd->qhgd", probs_low, value_rows, preferred_element_type=F32)
    mixed = mixed.astype(BF16).reshape(slots, QUERY_HEADS * HEAD_SIZE)
    hidden = tokens + jnp.dot(mixed, full_out, preferred_element_type=F32)
    normed_float_two, norm_two_pull = jax.vjp(rms_scale, hidden, full_gain_moe)
    normed_two = normed_float_two.astype(BF16)

    tok_ring = ring_gather(normed_two, order)
    gates = chosen_gates(
        jnp.dot(normed_two, full_router, preferred_element_type=F32)[:, :experts], table
    )
    valid_rows = (rows_index < length)[:, None]
    grad_y = jnp.where(valid_rows, cotangent[0].astype(F32), 0.0)

    near = (groups - 1) // 2
    arrivals = [(0,)] + [(-s, s) for s in range(1, near + 1)]
    if groups % 2 == 0:
        arrivals.append((groups // 2,))
    order_array = jnp.asarray(order, jnp.int32)
    first = (me * local).astype(jnp.int32).reshape(1)
    out_parts, grad_parts, gate_dots, kept, start = {}, {}, {}, (), 0
    for offsets in arrivals:
        seqs = order_array[(my_place + jnp.asarray(offsets, jnp.int32)) % groups]
        tok = jnp.stack([tok_ring[s] for s in offsets])
        cot = jnp.stack([cot_ring[s] for s in offsets])
        part_out, part_grad, dots, *kept = run_experts(
            first, seqs, tok, cot, row_tables, col_tables, full_router, w_gate, w_up, w_down,
            padded, kept, start, groups,
        )
        for j, s in enumerate(offsets):
            out_parts[s] = part_out[j]
            grad_parts[s] = part_grad[j]
            gate_dots[s % groups] = dots[j, :, :local].T
        start += len(offsets)
    rows_all, geo_all, inner_all, ggp_all, gup_all = kept

    by_offset = jnp.stack([gate_dots[s] for s in range(groups)])
    natural = by_offset[(jnp.asarray(place_of, jnp.int32) - my_place) % groups]
    grad_gates = lax.all_to_all(natural, "fsdp", split_axis=0, concat_axis=0, tiled=True)
    grad_gates = grad_gates.reshape(experts, slots).T

    left, right = ring_scatter(grad_parts, order)
    grad_normed_two = grad_parts[0].astype(F32) + left.astype(F32) + right.astype(F32)

    grad_down = jnp.einsum("necf,necd->efd", inner_all, geo_all, preferred_element_type=F32)
    grad_gate = jnp.einsum("necd,necf->edf", rows_all, ggp_all, preferred_element_type=F32)
    grad_up = jnp.einsum("necd,necf->edf", rows_all, gup_all, preferred_element_type=F32)
    expert_grads = [lax.psum(g.astype(BF16), "rep").astype(F32) for g in (grad_gate, grad_up, grad_down)]

    grad_logits = gates * (grad_gates - jnp.sum(gates * grad_gates, axis=-1, keepdims=True))
    grad_logits = grad_logits.astype(BF16)
    grad_normed_two = grad_normed_two + jnp.einsum(
        "se,de->sd", grad_logits, full_router[:, :experts], preferred_element_type=F32
    )
    grad_router = jnp.einsum("sd,se->de", normed_two, grad_logits, preferred_element_type=F32)
    grad_hidden_norm, grad_gain_moe = norm_two_pull(grad_normed_two)
    grad_hidden = grad_y + grad_hidden_norm
    grad_attn = grad_hidden.astype(BF16)
    grad_out = jnp.einsum("sa,sd->ad", mixed, grad_attn, preferred_element_type=F32)

    def reduce_weight(grad):
        owned = lax.psum_scatter(grad.astype(BF16), ALL, scatter_dimension=0, tiled=True)
        return lax.all_gather(owned, "rep", axis=0, tiled=True)

    total_out = reduce_weight(grad_out).astype(F32)
    out_left, out_right = ring_scatter(out_parts, order)
    mixture = out_parts[0].astype(F32) + out_left.astype(F32) + out_right.astype(F32)
    output = jnp.where(valid_rows, hidden + mixture, 0.0).astype(BF16)

    gradient_mixed_rows = jnp.einsum("sd,ad->sa", grad_attn, full_out, preferred_element_type=F32)
    gradient_mixed_rows = gradient_mixed_rows.astype(BF16).reshape(
        slots, KEY_VALUE_HEADS, group_width, HEAD_SIZE
    )
    scores = masked_scores()
    probs = jnp.exp(scores - log_total)
    probs_low = probs.astype(BF16)
    gradient_value_rows = jnp.einsum(
        "hgqk,qhgd->khd", probs_low, gradient_mixed_rows, preferred_element_type=F32
    )
    gradient_value_rows = gradient_value_rows.astype(BF16).reshape(slots, k_width)
    grad_probs = jnp.einsum(
        "qhgd,khd->hgqk", gradient_mixed_rows, value_rows, preferred_element_type=F32
    )
    grad_scores = probs * (grad_probs - jnp.sum(probs * grad_probs, axis=-1, keepdims=True))
    grad_scores = grad_scores.astype(BF16)
    grad_rot_queries = (
        jnp.einsum("hgqk,khd->qhgd", grad_scores, rot_keys, preferred_element_type=F32)
        * scale_factor
    )
    gradient_rotated_keys = (
        jnp.einsum("hgqk,qhgd->khd", grad_scores, rot_queries, preferred_element_type=F32)
        * scale_factor
    )
    grad_queries = (
        rotary_apply(grad_rot_queries, cosine_table, -sine_table).astype(BF16).reshape(slots, q_width)
    )
    grad_keys = (
        rotary_apply(gradient_rotated_keys, cosine_table, -sine_table)
        .astype(BF16)
        .reshape(slots, k_width)
    )
    grad_projected = jnp.concatenate([grad_queries, grad_keys, gradient_value_rows], axis=1)
    grad_qkv = jnp.einsum("sd,sa->da", attention_normed, grad_projected, preferred_element_type=F32)
    grad_normed_one = jnp.einsum("sa,da->sd", grad_projected, full_qkv, preferred_element_type=F32)
    grad_tokens_norm, grad_gain_attn = norm_one_pull(grad_normed_one)
    grad_input = (grad_hidden + grad_tokens_norm).astype(BF16)
    grad_small = jnp.concatenate(
        [
            grad_router,
            grad_gain_attn[:, None],
            grad_gain_moe[:, None],
            jnp.zeros((width, SMALL - experts - 2), F32),
        ],
        axis=1,
    )
    total_first = reduce_weight(jnp.concatenate([grad_qkv, grad_small], axis=1)).astype(F32)
    total_small = total_first[:, q_width + 2 * k_width :]
    return (
        output[None],
        grad_input[None],
        total_small[:, experts],
        total_small[:, experts + 1],
        total_first[:, :q_width],
        total_first[:, q_width : q_width + k_width],
        total_first[:, q_width + k_width : q_width + 2 * k_width],
        total_out,
        total_small[:, :experts],
        *expert_grads,
    )


def solution(mesh):
    in_specs = (
        P(("rep", "fsdp"), None, None),
        P(("rep", "fsdp"), None, None),
        P(("rep", "fsdp")),
        P(("rep", "fsdp"), None, None),
        P("fsdp"),
        P("fsdp"),
        P("fsdp", None),
        P("fsdp", None),
        P("fsdp", None),
        P("fsdp", None),
        P("fsdp", None),
        P("fsdp", None, None),
        P("fsdp", None, None),
        P("fsdp", None, None),
    )
    out_specs = (
        P(("rep", "fsdp"), None, None),
        P(("rep", "fsdp"), None, None),
        P("fsdp"),
        P("fsdp"),
        P("fsdp", None),
        P("fsdp", None),
        P("fsdp", None),
        P("fsdp", None),
        P("fsdp", None),
        P("fsdp", None, None),
        P("fsdp", None, None),
        P("fsdp", None, None),
    )
    return jax.shard_map(body, mesh=mesh, in_specs=in_specs, out_specs=out_specs, check_vma=False)
```

```python
import functools
import math

import jax
import jax.numpy as jnp
from jax import lax
from jax.experimental import pallas as pl
from jax.experimental.pallas import tpu as pltpu
from jax.sharding import PartitionSpec as P

QUERY_HEADS = 24
KEY_VALUE_HEADS = 8
HEAD_SIZE = 64
BF16 = jnp.bfloat16
F32 = jnp.float32
ALL = ("fsdp", "rep")
SMALL = 128
LIGHT = pl.CostEstimate(flops=1000, bytes_accessed=1000, transcendentals=0)


def rms_scale(value_rows, gain_vec):
    inverse = lax.rsqrt(jnp.mean(value_rows * value_rows, axis=-1, keepdims=True) + 1e-05)
    return value_rows * inverse * gain_vec


def rotation(expert_slot_count, head_dim):
    half_dim = head_dim // 2
    frequency = jnp.exp(
        -jnp.log(10000.0) * 2.0 * jnp.arange(half_dim, dtype=jnp.float32) / head_dim
    )
    angles = jnp.arange(expert_slot_count, dtype=jnp.float32)[:, None] * frequency[None, :]
    return (jnp.cos(angles), jnp.sin(angles))


def slot_table(choices_row, length, experts, capacity):
    slots = choices_row.shape[0]
    valid = (jnp.arange(slots, dtype=jnp.int32) < length)[:, None]
    chosen = jnp.any(
        choices_row[:, :, None] == jnp.arange(experts, dtype=jnp.int32)[None, None, :], axis=1
    )
    hit = (chosen & valid).astype(F32)
    rows = jnp.arange(slots, dtype=jnp.int32)
    earlier = (rows[None, :] < rows[:, None]).astype(BF16)
    position = jnp.dot(earlier, hit.astype(BF16), preferred_element_type=F32).astype(jnp.int32)
    kept = chosen & valid & (position < capacity)
    return jnp.where(kept, position, jnp.where(chosen, -1, -2))


def chosen_gates(logits, table):
    chosen = table >= -1
    masked = jnp.where(chosen, logits, -1e30)
    top = jnp.max(masked, axis=-1, keepdims=True)
    raised = jnp.where(chosen, jnp.exp(masked - top), 0.0)
    return raised / jnp.sum(raised, axis=-1, keepdims=True)


def ring_order(size):
    if size % 2:
        return list(range(size))
    return list(range(0, size, 2)) + list(range(size - 1, 0, -2))


def tie(values, deps):
    anywhere = pl.BlockSpec(memory_space=pl.ANY)
    return pl.pallas_call(
        lambda *refs: None,
        out_shape=[jax.ShapeDtypeStruct(v.shape, v.dtype) for v in values],
        in_specs=[anywhere] * (len(values) + len(deps)),
        out_specs=[anywhere] * len(values),
        input_output_aliases={i: i for i in range(len(values))},
        cost_estimate=LIGHT,
    )(*values, *deps)


def swap(value, axis, bit):
    size = lax.axis_size(axis)
    return lax.ppermute(value, axis, [(i, i ^ bit) for i in range(size)])


def shift(value, order, step):
    size = len(order)
    return lax.ppermute(value, "fsdp", [(order[i], order[(i + step) % size]) for i in range(size)])


def ring_start(value, order, steps):
    found = {0: value}
    for step in range(1, min(steps, (len(order) - 1) // 2) + 1):
        found[-step] = shift(found[1 - step], order, 1)
        found[step] = shift(found[step - 1], order, -1)
    return found


def ring_finish(found, order, deps):
    size = len(order)
    found = dict(found)
    reach = max(found)
    back, ahead = found[-reach], found[reach]
    if deps:
        back, ahead = tie([back, ahead], deps)
    for step in range(reach + 1, (size - 1) // 2 + 1):
        back = shift(back, order, 1)
        ahead = shift(ahead, order, -1)
        found[-step] = back
        found[step] = ahead
    if size % 2 == 0:
        half = back.shape[0] // 2
        top = shift(back[:half], order, 1)
        bottom = shift(ahead[half:], order, -1)
        found[size // 2] = jnp.concatenate([top, bottom], axis=0)
    return found


def add_low(left, right):
    return (left.astype(F32) + right.astype(F32)).astype(BF16)


def ring_scatter(parts, order):
    size = len(order)
    near = (size - 1) // 2
    if size % 2 == 0:
        far = parts[size // 2]
        half = far.shape[0] // 2
        top = shift(far[:half], order, 1)
        bottom = shift(far[half:], order, -1)
        ahead, back = parts[near], parts[-near]
        ahead = jnp.concatenate([add_low(ahead[:half], top), ahead[half:]], axis=0)
        back = jnp.concatenate([back[:half], add_low(back[half:], bottom)], axis=0)
    else:
        ahead, back = parts[near], parts[-near]
    stages = [[ahead, back]]
    for step in range(near, 0, -1):
        ahead = shift(ahead, order, 1)
        back = shift(back, order, -1)
        if step > 1:
            ahead = add_low(parts[step - 1], ahead)
            back = add_low(parts[1 - step], back)
        stages.append([ahead, back])
    return ahead, back, stages


def three_way(value):
    high = value.astype(BF16)
    rest = value - high.astype(F32)
    middle = rest.astype(BF16)
    low = (rest - middle.astype(F32)).astype(BF16)
    return high, middle, low


def dot_nn(left, right):
    return jnp.dot(left, right, preferred_element_type=F32)


def dot_nt(left, right):
    return lax.dot_general(left, right, (((1,), (1,)), ((), ())), preferred_element_type=F32)


def dot_tn(left, right):
    return lax.dot_general(left, right, (((0,), (0,)), ((), ())), preferred_element_type=F32)


def tile_rotate(value, cosine, sine_left, sine_right):
    tiles = []
    for start in range(0, value.shape[1], SMALL):
        tile = value[:, start : start + SMALL]
        ahead = pltpu.roll(tile, SMALL - HEAD_SIZE // 2, axis=1)
        behind = pltpu.roll(tile, HEAD_SIZE // 2, axis=1)
        tiles.append(tile * cosine + ahead * sine_left + behind * sine_right)
    return jnp.concatenate(tiles, axis=1)


def half_variants(tile):
    lanes = lax.broadcasted_iota(jnp.int32, tile.shape, 1)
    wide = tile.astype(F32)
    turned = pltpu.roll(wide, HEAD_SIZE, axis=1)
    pick = lambda source, half: jnp.where((lanes >= HEAD_SIZE) == (half == 1), source, 0.0).astype(BF16)
    return {(c, a): pick(wide if c == a else turned, a) for c in range(2) for a in range(2)}


def row_blocks(slots):
    size = min(256, slots)
    return [(start, size, start + size) for start in range(0, slots, size)]


def allowed_block(start, size, keys, length):
    query = start + lax.broadcasted_iota(jnp.int32, (size, keys), 0)
    key = lax.broadcasted_iota(jnp.int32, (size, keys), 1)
    return (key <= query) & (key < length)


def attention_kernel(
    length_ref, x_ref, wq_ref, wk_ref, wv_ref, cos_ref, left_ref, right_ref, *rest
):
    q_ref, k_ref, v_ref, mixed_ref, lse_ref = rest[-5:]
    x = x_ref[...]
    slots = x.shape[0]
    tables = (cos_ref[...], left_ref[...], right_ref[...])
    q = tile_rotate(dot_nn(x, wq_ref[...]), *tables).astype(BF16)
    k = tile_rotate(dot_nn(x, wk_ref[...]), *tables).astype(BF16)
    v = dot_nn(x, wv_ref[...]).astype(BF16)
    q_ref[...] = q
    k_ref[...] = k
    v_ref[...] = v
    keys, values = half_variants(k), half_variants(v)
    heads = q.shape[1] // HEAD_SIZE
    group = heads // 2
    scale = 1.0 / math.sqrt(HEAD_SIZE)
    for start, size, seen in row_blocks(slots):
        allowed = allowed_block(start, size, seen, length_ref[0])
        lanes = lax.broadcasted_iota(jnp.int32, (size, SMALL), 1)
        lse = jnp.zeros((size, SMALL), F32)
        for tile in range(heads // 2):
            q_tile = q[start : start + size, tile * SMALL : (tile + 1) * SMALL]
            total = jnp.zeros((size, SMALL), F32)
            for half in range(2):
                head = 2 * tile + half
                which = (head // group, half)
                scores = dot_nt(q_tile, keys[which][:seen]) * scale
                scores = jnp.where(allowed, scores, -1e30)
                top = jnp.max(scores, axis=1, keepdims=True)
                raised = jnp.exp(scores - top)
                mass = jnp.sum(raised, axis=1, keepdims=True)
                probs = (raised * (1.0 / mass)).astype(BF16)
                total = total + dot_nn(probs, values[which][:seen])
                lse = jnp.where(lanes == head, top + jnp.log(mass), lse)
            mixed_ref[start : start + size, tile * SMALL : (tile + 1) * SMALL] = total.astype(BF16)
        lse_ref[0, start : start + size] = lse


def attention_back_kernel(
    length_ref, ga_ref, wo_ref, q_ref, k_ref, v_ref, lse_ref, cos_ref, left_ref, right_ref, *rest
):
    gq_ref, gk_ref, gv_ref = rest[-3:]
    slots = ga_ref.shape[0]
    q, k, v = q_ref[...], k_ref[...], v_ref[...]
    grad_mixed = dot_nt(ga_ref[...], wo_ref[...]).astype(BF16)
    keys, values = half_variants(k), half_variants(v)
    heads = q.shape[1] // HEAD_SIZE
    group = heads // 2
    scale = 1.0 / math.sqrt(HEAD_SIZE)
    blocks = row_blocks(slots)
    pairs = [(c, a) for c in range(2) for a in range(2)]
    zero = lambda: [jnp.zeros((size, SMALL), F32) for _, size, _ in blocks]
    gk, gv = {p: zero() for p in pairs}, {p: zero() for p in pairs}
    turn = (cos_ref[...], -left_ref[...], -right_ref[...])
    for start, size, seen in blocks:
        allowed = allowed_block(start, size, seen, length_ref[0])
        rows = slice(start, start + size)
        for tile in range(heads // 2):
            columns = slice(tile * SMALL, (tile + 1) * SMALL)
            q_tile, g_tile = q[rows, columns], grad_mixed[rows, columns]
            total = jnp.zeros((size, SMALL), F32)
            for half in range(2):
                head = 2 * tile + half
                which = (head // group, half)
                scores = dot_nt(q_tile, keys[which][:seen]) * scale
                probs = jnp.where(allowed, jnp.exp(scores - lse_ref[0, rows, head : head + 1]), 0.0)
                grad_probs = dot_nt(g_tile, values[which][:seen])
                weighted = probs * grad_probs
                grad_scores = weighted - probs * jnp.sum(weighted, axis=1, keepdims=True)
                grad_scores = grad_scores.astype(BF16)
                probs_low = probs.astype(BF16)
                total = total + dot_nn(grad_scores, keys[which][:seen])
                gv_part = dot_tn(probs_low, g_tile)
                gk_part = dot_tn(grad_scores, q_tile)
                for b, (key_start, key_size, _) in enumerate(blocks):
                    if key_start < seen:
                        piece = slice(key_start, key_start + key_size)
                        gv[which][b] = gv[which][b] + gv_part[piece]
                        gk[which][b] = gk[which][b] + gk_part[piece]
            turned = tile_rotate(total * scale, *[t[rows] for t in turn])
            gq_ref[rows, columns] = turned.astype(BF16)

    for b, (start, size, _) in enumerate(blocks):
        rows = slice(start, start + size)
        lanes = lax.broadcasted_iota(jnp.int32, (size, SMALL), 1)
        right = lanes >= HEAD_SIZE

        def joined(parts):
            placed = []
            for c in range(2):
                kept = parts[(c, c)][b]
                moved = pltpu.roll(parts[(c, 1 - c)][b], HEAD_SIZE, axis=1)
                placed.append(kept + moved)
            return jnp.where(right, placed[1], placed[0])

        gv_ref[rows] = joined(gv).astype(BF16)
        gk_ref[rows] = tile_rotate(joined(gk) * scale, *[t[rows] for t in turn]).astype(BF16)


def rotary_tables(slots):
    cosine, sine = rotation(slots, HEAD_SIZE)
    zero = jnp.zeros_like(sine)
    tile = lambda left, right: jnp.concatenate([left, right] * (SMALL // HEAD_SIZE), axis=1)
    return tile(cosine, cosine), tile(-sine, zero), tile(zero, sine)


def head_steps(k_width):
    return k_width // SMALL


def attention(length, normed, weights, tables, q_width, k_width, deps):
    slots, width = normed.shape
    steps = head_steps(k_width)
    q_block = q_width // steps
    fixed = lambda j, n: (0, 0)
    shapes = [(slots, q_width), (slots, k_width), (slots, k_width), (slots, q_width)]
    return pl.pallas_call(
        attention_kernel,
        out_shape=[jax.ShapeDtypeStruct(s, BF16) for s in shapes]
        + [jax.ShapeDtypeStruct((steps, slots, SMALL), F32)],
        grid_spec=pltpu.PrefetchScalarGridSpec(
            num_scalar_prefetch=1,
            grid=(steps,),
            in_specs=[
                pl.BlockSpec((slots, width), fixed),
                pl.BlockSpec((width, q_block), lambda j, n: (0, j)),
                pl.BlockSpec((width, SMALL), lambda j, n: (0, q_width // SMALL + j)),
                pl.BlockSpec((width, SMALL), lambda j, n: (0, (q_width + k_width) // SMALL + j)),
                pl.BlockSpec((slots, SMALL), fixed),
                pl.BlockSpec((slots, SMALL), fixed),
                pl.BlockSpec((slots, SMALL), fixed),
            ]
            + [pl.BlockSpec(memory_space=pl.ANY)] * len(deps),
            out_specs=[
                pl.BlockSpec((slots, q_block), lambda j, n: (0, j)),
                pl.BlockSpec((slots, SMALL), lambda j, n: (0, j)),
                pl.BlockSpec((slots, SMALL), lambda j, n: (0, j)),
                pl.BlockSpec((slots, q_block), lambda j, n: (0, j)),
                pl.BlockSpec((1, slots, SMALL), lambda j, n: (j, 0, 0)),
            ],
        ),
        compiler_params=pltpu.CompilerParams(
            dimension_semantics=("arbitrary",), vmem_limit_bytes=48 * 1024 * 1024
        ),
        cost_estimate=pl.CostEstimate(flops=25 * 10**9, bytes_accessed=10**7, transcendentals=10**7),
    )(length.reshape(1), normed, weights, weights, weights, *tables, *deps)


def attention_back(length, grad_attn, w_out, q, k, v, lse, tables, deps):
    slots, width = grad_attn.shape
    q_width, k_width = q.shape[1], k.shape[1]
    steps = head_steps(k_width)
    q_block = q_width // steps
    fixed = lambda j, n: (0, 0)
    shapes = [(slots, q_width), (slots, k_width), (slots, k_width)]
    q_spec = pl.BlockSpec((slots, q_block), lambda j, n: (0, j))
    k_spec = pl.BlockSpec((slots, SMALL), lambda j, n: (0, j))
    return pl.pallas_call(
        attention_back_kernel,
        out_shape=[jax.ShapeDtypeStruct(s, BF16) for s in shapes],
        grid_spec=pltpu.PrefetchScalarGridSpec(
            num_scalar_prefetch=1,
            grid=(steps,),
            in_specs=[
                pl.BlockSpec((slots, width), fixed),
                pl.BlockSpec((q_block, width), lambda j, n: (j, 0)),
                q_spec,
                k_spec,
                k_spec,
                pl.BlockSpec((1, slots, SMALL), lambda j, n: (j, 0, 0)),
                pl.BlockSpec((slots, SMALL), fixed),
                pl.BlockSpec((slots, SMALL), fixed),
                pl.BlockSpec((slots, SMALL), fixed),
            ]
            + [pl.BlockSpec(memory_space=pl.ANY)] * len(deps),
            out_specs=[q_spec, k_spec, k_spec],
        ),
        compiler_params=pltpu.CompilerParams(
            dimension_semantics=("arbitrary",), vmem_limit_bytes=48 * 1024 * 1024
        ),
        cost_estimate=pl.CostEstimate(flops=3 * 10**10, bytes_accessed=10**7, transcendentals=10**7),
    )(length.reshape(1), grad_attn, w_out, q, k, v, lse, *tables, *deps)


def out_kernel(mixed_ref, weight_ref, input_ref, gain_ref, *rest):
    hidden_ref, normed_ref = rest[-2:]
    hidden = input_ref[...].astype(F32) + dot_nn(mixed_ref[...], weight_ref[...])
    hidden_ref[...] = hidden
    normed_ref[...] = rms_scale(hidden, gain_ref[...]).astype(BF16)


def attention_out(mixed, weights, inputs, gain, deps, rows=128):
    slots, width = inputs.shape
    q_width = mixed.shape[1]
    spec = pl.BlockSpec((rows, width), lambda i: (i, 0))
    return pl.pallas_call(
        out_kernel,
        out_shape=[
            jax.ShapeDtypeStruct((slots, width), F32),
            jax.ShapeDtypeStruct((slots, width), BF16),
        ],
        grid=(slots // rows,),
        in_specs=[
            pl.BlockSpec((rows, q_width), lambda i: (i, 0)),
            pl.BlockSpec((q_width, width), lambda i: (0, 0)),
            spec,
            pl.BlockSpec((1, width), lambda i: (0, 0)),
        ]
        + [pl.BlockSpec(memory_space=pl.ANY)] * len(deps),
        out_specs=[spec, spec],
        compiler_params=pltpu.CompilerParams(
            dimension_semantics=("arbitrary",), vmem_limit_bytes=40 * 1024 * 1024
        ),
        cost_estimate=LIGHT,
    )(mixed, weights, inputs, gain.reshape(1, width), *deps)


def joint_grad_kernel(left_a_ref, right_a_ref, left_b_ref, right_b_ref, out_ref, *, steps):
    first = pl.program_id(0) < steps

    @pl.when(first)
    def _():
        out_ref[...] = dot_tn(left_a_ref[...], right_a_ref[...]).astype(BF16)

    @pl.when(jnp.logical_not(first))
    def _():
        out_ref[...] = dot_tn(left_b_ref[...], right_b_ref[...]).astype(BF16)


def joint_grad(left_a, right_a, left_b, right_b, columns=512):
    slots, rows = left_a.shape
    steps = right_a.shape[1] // columns
    width = right_a.shape[1] + right_b.shape[1]
    whole = pl.BlockSpec((slots, rows), lambda j: (0, 0))
    return pl.pallas_call(
        functools.partial(joint_grad_kernel, steps=steps),
        out_shape=jax.ShapeDtypeStruct((rows, width), BF16),
        grid=(width // columns,),
        in_specs=[
            whole,
            pl.BlockSpec((slots, columns), lambda j: (0, jnp.minimum(j, steps - 1))),
            whole,
            pl.BlockSpec((slots, columns), lambda j: (0, jnp.maximum(j - steps, 0))),
        ],
        out_specs=pl.BlockSpec((rows, columns), lambda j: (0, j)),
        compiler_params=pltpu.CompilerParams(
            dimension_semantics=("arbitrary",), vmem_limit_bytes=48 * 1024 * 1024
        ),
        cost_estimate=LIGHT,
    )(left_a, right_a, left_b, right_b)


def expert_kernel(
    first_ref,
    seq_ref,
    tok_ref,
    cot_ref,
    row_ref,
    col_ref,
    router_ref,
    gate_ref,
    up_ref,
    down_ref,
    *rest,
    padded,
):
    (
        out_ref,
        grad_ref,
        gg_ref,
        rows_ref,
        geo_ref,
        inner_ref,
        ggp_ref,
        gup_ref,
        gates_scr,
        out_acc,
        grad_acc,
    ) = rest[-11:]
    e = pl.program_id(1)
    tok = tok_ref[0]
    cot = cot_ref[0]
    slots = tok.shape[0]
    table = col_ref[0]
    lanes = lax.broadcasted_iota(jnp.int32, table.shape, 1)

    @pl.when(e == 0)
    def _():
        gates_scr[...] = chosen_gates(dot_nn(tok, router_ref[...]), table)
        out_acc[...] = jnp.zeros_like(out_acc)
        grad_acc[...] = jnp.zeros_like(grad_acc)
        gg_ref[0] = jnp.zeros_like(gg_ref[0])

    mine = lanes == first_ref[0] + e
    gate_lane = jnp.where(mine, gates_scr[...], 0.0)
    gate_col = jnp.sum(gate_lane, axis=1, keepdims=True)
    pos_col = jnp.sum(jnp.where(mine, table.astype(F32), 0.0), axis=1, keepdims=True).astype(jnp.int32)
    pos_row = row_ref[0, 0]
    pick = (lax.broadcasted_iota(jnp.int32, (padded, slots), 0) == pos_row).astype(F32).astype(BF16)
    place = (lax.broadcasted_iota(jnp.int32, (slots, padded), 1) == pos_col).astype(F32).astype(BF16)

    rows = dot_nn(pick, tok).astype(BF16)
    cot_rows = dot_nn(pick, cot)
    high, middle, low = three_way(gate_lane)
    gate_slot = dot_nn(pick, high) + dot_nn(pick, middle) + dot_nn(pick, low)
    gate_slot = jnp.sum(gate_slot, axis=1, keepdims=True)
    rows_ref[0, 0] = rows

    gate_part = dot_nn(rows, gate_ref[0])
    up_part = dot_nn(rows, up_ref[0])
    sig = 1.0 / (1.0 + jnp.exp(-gate_part))
    silu = gate_part * sig
    inner = (silu * up_part).astype(BF16)
    inner_ref[0, 0] = inner
    expert_out = dot_nn(inner, down_ref[0]).astype(BF16)
    out_acc[...] += gate_col * dot_nn(place, expert_out)

    dots = jnp.sum(cot_rows * expert_out.astype(F32), axis=1, keepdims=True)
    spread = jnp.where(lax.broadcasted_iota(jnp.int32, (padded, SMALL), 1) == e, dots, 0.0)
    high, middle, low = three_way(spread)
    gg_ref[0] += dot_nn(place, high) + dot_nn(place, middle) + dot_nn(place, low)

    geo = (gate_slot * cot_rows).astype(BF16)
    geo_ref[0, 0] = geo
    grad_inner = dot_nt(geo, down_ref[0])
    ggp = (grad_inner * up_part * sig * (1.0 + gate_part * (1.0 - sig))).astype(BF16)
    gup = (grad_inner * silu).astype(BF16)
    ggp_ref[0, 0] = ggp
    gup_ref[0, 0] = gup
    grad_rows = (dot_nt(ggp, gate_ref[0]) + dot_nt(gup, up_ref[0])).astype(BF16)
    grad_acc[...] += dot_nn(place, grad_rows)

    @pl.when(e == pl.num_programs(1) - 1)
    def _():
        out_ref[0] = out_acc[...].astype(BF16)
        grad_ref[0] = grad_acc[...].astype(BF16)


def run_experts(first, seqs, tok, cot, rows_table, cols_table, router, w_gate, w_up, w_down, padded, kept, start, total):
    count, slots, width = tok.shape
    local, _, ff = w_gate.shape
    row_block = lambda s, e, first, seq: (seq[s], first[0] + e, 0, 0)
    col_block = lambda s, e, first, seq: (seq[s], 0, 0)
    seq_block = lambda s, e, first, seq: (s, 0, 0)
    slot_block = lambda s, e, first, seq: (start + s, e, 0, 0)
    expert_block = lambda s, e, first, seq: (e, 0, 0)
    wide = jax.ShapeDtypeStruct((total, local, padded, width), BF16)
    thin = jax.ShapeDtypeStruct((total, local, padded, ff), BF16)
    whole = jax.ShapeDtypeStruct((count, slots, width), BF16)
    flops = 2 * count * local * (padded * width * (6 * ff + 4 * slots))
    moved = 4 * count * slots * width * 2 + count * local * (3 * width * ff + padded * (2 * width + 3 * ff)) * 2
    return pl.pallas_call(
        functools.partial(expert_kernel, padded=padded),
        out_shape=(
            whole,
            whole,
            jax.ShapeDtypeStruct((count, slots, SMALL), F32),
            wide,
            wide,
            thin,
            thin,
            thin,
        ),
        grid_spec=pltpu.PrefetchScalarGridSpec(
            num_scalar_prefetch=2,
            grid=(count, local),
            in_specs=[
                pl.BlockSpec((1, slots, width), seq_block),
                pl.BlockSpec((1, slots, width), seq_block),
                pl.BlockSpec((1, 1, 1, slots), row_block),
                pl.BlockSpec((1, slots, SMALL), col_block),
                pl.BlockSpec((width, SMALL), lambda s, e, first, seq: (0, 0)),
                pl.BlockSpec((1, width, ff), expert_block),
                pl.BlockSpec((1, width, ff), expert_block),
                pl.BlockSpec((1, ff, width), expert_block),
            ]
            + [pl.BlockSpec(memory_space=pl.ANY)] * len(kept),
            out_specs=[
                pl.BlockSpec((1, slots, width), seq_block),
                pl.BlockSpec((1, slots, width), seq_block),
                pl.BlockSpec((1, slots, SMALL), seq_block),
                pl.BlockSpec((1, 1, padded, width), slot_block),
                pl.BlockSpec((1, 1, padded, width), slot_block),
                pl.BlockSpec((1, 1, padded, ff), slot_block),
                pl.BlockSpec((1, 1, padded, ff), slot_block),
                pl.BlockSpec((1, 1, padded, ff), slot_block),
            ],
            scratch_shapes=[
                pltpu.VMEM((slots, SMALL), F32),
                pltpu.VMEM((slots, width), F32),
                pltpu.VMEM((slots, width), F32),
            ],
        ),
        input_output_aliases={10 + i: 3 + i for i in range(len(kept))},
        compiler_params=pltpu.CompilerParams(
            dimension_semantics=("arbitrary", "arbitrary"), vmem_limit_bytes=58 * 1024 * 1024
        ),
        cost_estimate=pl.CostEstimate(flops=flops, bytes_accessed=moved, transcendentals=count * local * padded * ff),
    )(first, seqs, tok, cot, rows_table, cols_table, router, w_gate, w_up, w_down, *kept)


def body(
    inputs,
    cotangent,
    lengths,
    choices,
    gain_attn,
    gain_moe,
    query_weight,
    key_weight,
    value_weight,
    w_out,
    w_router,
    w_gate,
    w_up,
    w_down,
):
    groups = lax.axis_size("fsdp")
    replicas = lax.axis_size("rep")
    me = lax.axis_index("fsdp")
    rep = lax.axis_index("rep")
    tokens = inputs[0].astype(F32)
    slots, width = tokens.shape
    length = lengths[0]
    choices_row = choices[0]
    top_count = choices_row.shape[1]
    local = w_gate.shape[0]
    experts = local * groups
    capacity = 25 * slots * top_count // (32 * experts)
    padded = -(-capacity // 16) * 16
    q_width = query_weight.shape[1]
    k_width = key_weight.shape[1]
    tables = rotary_tables(slots)
    order = ring_order(groups)
    place_of = [order.index(j) for j in range(groups)]
    my_place = jnp.asarray(place_of, jnp.int32)[me]

    small = jnp.concatenate(
        [
            w_router,
            gain_attn[:, None],
            gain_moe[:, None],
            jnp.zeros((w_router.shape[0], SMALL - experts - 2), BF16),
        ],
        axis=1,
    )
    share = query_weight.shape[0] // replicas

    def gather_weight(shard):
        piece = lax.dynamic_slice_in_dim(shard, rep * share, share, axis=0)
        return lax.all_gather(piece, ALL, axis=0, tiled=True)

    first_set = gather_weight(
        jnp.concatenate([query_weight, key_weight, value_weight, small], axis=1)
    )
    full_qkv = first_set[:, : q_width + 2 * k_width]
    full_small = first_set[:, q_width + 2 * k_width :]
    full_out = gather_weight(w_out)
    full_gain_attn = full_small[:, experts].astype(F32)
    full_gain_moe = full_small[:, experts + 1].astype(F32)
    lane = jnp.arange(SMALL)[None, :]
    full_router = jnp.where(lane < experts, full_small, jnp.zeros_like(full_small))

    table = slot_table(choices_row, length, experts, capacity)
    row_tables = table.T[None]
    bit = 1
    while bit < groups:
        other = swap(row_tables, "fsdp", bit)
        upper = jnp.bitwise_and(me // bit, 1) == 1
        row_tables = jnp.where(
            upper, jnp.concatenate([other, row_tables]), jnp.concatenate([row_tables, other])
        )
        bit *= 2
    col_tables = jnp.pad(
        jnp.swapaxes(row_tables, 1, 2), ((0, 0), (0, 0), (0, SMALL - experts)), constant_values=-2
    )
    row_tables = row_tables[:, :, None, :]
    cot_ring = ring_start(tie([cotangent[0]], [row_tables])[0], order, 2)

    normed_float, norm_one_pull = jax.vjp(rms_scale, tokens, full_gain_attn)
    attention_normed = normed_float.astype(BF16)
    rot_queries, rot_keys, value_rows, mixed, log_total = attention(
        length, attention_normed, first_set, tables, q_width, k_width, [row_tables, col_tables]
    )
    rows_index = jnp.arange(slots, dtype=jnp.int32)
    near_cot = [cot_ring[o] for o in (1, -1, 2, -2) if o in cot_ring]
    cot_ring = ring_finish(cot_ring, order, [mixed])
    hidden, normed_two = attention_out(
        mixed, full_out, inputs[0], full_gain_moe, near_cot
    )
    norm_two_pull = jax.vjp(rms_scale, hidden, full_gain_moe)[1]

    tok_ring = ring_finish(ring_start(normed_two, order, 1), order, [])
    gates = chosen_gates(
        jnp.dot(normed_two, full_router, preferred_element_type=F32)[:, :experts], table
    )
    valid_rows = (rows_index < length)[:, None]
    grad_y = jnp.where(valid_rows, cotangent[0].astype(F32), 0.0)

    near = (groups - 1) // 2
    arrivals = [(0,)] + [(-s, s) for s in range(1, near + 1)]
    if groups % 2 == 0:
        arrivals.append((groups // 2,))
    order_array = jnp.asarray(order, jnp.int32)
    first = (me * local).astype(jnp.int32).reshape(1)
    out_parts, grad_parts, gate_dots, kept, start = {}, {}, {}, (), 0
    for offsets in arrivals:
        seqs = order_array[(my_place + jnp.asarray(offsets, jnp.int32)) % groups]
        tok = jnp.stack([tok_ring[s] for s in offsets])
        cot = jnp.stack([cot_ring[s] for s in offsets])
        part_out, part_grad, dots, *kept = run_experts(
            first, seqs, tok, cot, row_tables, col_tables, full_router, w_gate, w_up, w_down,
            padded, kept, start, groups,
        )
        for j, s in enumerate(offsets):
            out_parts[s] = part_out[j]
            grad_parts[s] = part_grad[j]
            gate_dots[s % groups] = dots[j, :, :local].T
        start += len(offsets)
    rows_all, geo_all, inner_all, ggp_all, gup_all = kept

    by_offset = jnp.stack([gate_dots[s] for s in range(groups)])
    natural = by_offset[(jnp.asarray(place_of, jnp.int32) - my_place) % groups]
    grad_gates = lax.all_to_all(natural, "fsdp", split_axis=0, concat_axis=0, tiled=True)
    grad_gates = grad_gates.reshape(experts, slots).T

    grad_down = jnp.einsum("necf,necd->efd", inner_all, geo_all, preferred_element_type=F32)
    grad_gate = jnp.einsum("necd,necf->edf", rows_all, ggp_all, preferred_element_type=F32)
    grad_up = jnp.einsum("necd,necf->edf", rows_all, gup_all, preferred_element_type=F32)
    core_bit = jnp.bitwise_and(rep, 1)
    expert_sums = []
    for grad in (grad_gate, grad_up, grad_down):
        pairs = grad.astype(BF16).reshape(local // 2, 2, *grad.shape[1:])
        mine = lax.dynamic_index_in_dim(pairs, core_bit, 1, keepdims=False)
        other = lax.dynamic_index_in_dim(pairs, 1 - core_bit, 1, keepdims=False)
        expert_sums.append(add_low(mine, swap(other, "rep", 1)))

    left, right, _ = ring_scatter(grad_parts, order)
    (own_grads,) = tie([grad_parts[0]], expert_sums)
    grad_normed_two = own_grads.astype(F32) + left.astype(F32) + right.astype(F32)

    grad_logits = gates * (grad_gates - jnp.sum(gates * grad_gates, axis=-1, keepdims=True))
    grad_logits = grad_logits.astype(BF16)
    grad_normed_two = grad_normed_two + jnp.einsum(
        "se,de->sd", grad_logits, full_router[:, :experts], preferred_element_type=F32
    )
    grad_router = jnp.einsum("sd,se->ed", normed_two, grad_logits, preferred_element_type=F32)
    grad_hidden_norm, grad_gain_moe = norm_two_pull(grad_normed_two)
    grad_hidden = grad_y + grad_hidden_norm
    grad_attn = grad_hidden.astype(BF16)

    def reduce_weight(grad):
        owned = lax.psum_scatter(grad.astype(BF16), ALL, scatter_dimension=0, tiled=True)
        return [lax.all_gather(p, "rep", axis=0, tiled=True) for p in jnp.split(owned, 2, axis=1)]

    keys = sorted(out_parts)
    held = dict(zip(keys, tie([out_parts[o] for o in keys], [grad_attn])))
    out_left, out_right, stages = ring_scatter(held, order)
    mixture = held[0].astype(F32) + out_left.astype(F32) + out_right.astype(F32)
    output = jnp.where(valid_rows, hidden + mixture, 0.0).astype(BF16)

    grad_queries, grad_keys, grad_values = attention_back(
        length, grad_attn, full_out, rot_queries, rot_keys, value_rows, log_total, tables, []
    )
    projected = jnp.concatenate([grad_queries, grad_keys, grad_values], axis=1)
    crossed = [add_low(expert_sums[0], swap(expert_sums[0], "rep", 2))]
    (projected,) = tie([projected], [*stages[0], *crossed])
    grad_qkv = joint_grad(attention_normed, projected, mixed, grad_attn)
    (projected,) = tie([projected], [grad_qkv, *stages[min(1, len(stages) - 1)]])
    grad_normed_one = jnp.einsum("sa,da->sd", projected, full_qkv, preferred_element_type=F32)
    grad_tokens_norm, grad_gain_attn = norm_one_pull(grad_normed_one)
    grad_input = (grad_hidden + grad_tokens_norm).astype(BF16)
    total_first = jnp.concatenate(reduce_weight(grad_qkv), axis=1).astype(F32)
    small_sum = jnp.concatenate([grad_router, grad_gain_attn[None], grad_gain_moe[None]], axis=0)
    (small_sum,) = tie([small_sum.astype(BF16)], stages[min(2, len(stages) - 1)])
    for axis, size in (("fsdp", groups), ("rep", replicas)):
        bit = 1
        while bit < size:
            small_sum = add_low(small_sum, swap(small_sum, axis, bit))
            bit *= 2
    small_sum = small_sum.astype(F32)
    small_sum = lax.dynamic_slice_in_dim(small_sum, me * gain_attn.shape[0], gain_attn.shape[0], axis=1)

    expert_grads = []
    for total in (*crossed, *[add_low(t, swap(t, "rep", 2)) for t in expert_sums[1:]]):
        bit = 4
        while bit < replicas:
            total = add_low(total, swap(total, "rep", bit))
            bit *= 2
        other = swap(total, "rep", 1)
        pair = jnp.where(core_bit == 0, jnp.stack([total, other], 1), jnp.stack([other, total], 1))
        expert_grads.append(pair.reshape(local, *total.shape[1:]).astype(F32))
    return (
        output[None],
        grad_input[None],
        small_sum[experts],
        small_sum[experts + 1],
        total_first[:, :q_width],
        total_first[:, q_width : q_width + k_width],
        total_first[:, q_width + k_width : q_width + 2 * k_width],
        total_first[:, q_width + 2 * k_width :],
        small_sum[:experts].T,
        *expert_grads,
    )


def solution(mesh):
    in_specs = (
        P(("rep", "fsdp"), None, None),
        P(("rep", "fsdp"), None, None),
        P(("rep", "fsdp")),
        P(("rep", "fsdp"), None, None),
        P("fsdp"),
        P("fsdp"),
        P("fsdp", None),
        P("fsdp", None),
        P("fsdp", None),
        P("fsdp", None),
        P("fsdp", None),
        P("fsdp", None, None),
        P("fsdp", None, None),
        P("fsdp", None, None),
    )
    out_specs = (
        P(("rep", "fsdp"), None, None),
        P(("rep", "fsdp"), None, None),
        P("fsdp"),
        P("fsdp"),
        P("fsdp", None),
        P("fsdp", None),
        P("fsdp", None),
        P("fsdp", None),
        P("fsdp", None),
        P("fsdp", None, None),
        P("fsdp", None, None),
        P("fsdp", None, None),
    )
    return jax.shard_map(body, mesh=mesh, in_specs=in_specs, out_specs=out_specs, check_vma=False)
```

```python
import functools
import math

import jax
import jax.numpy as jnp
from jax import lax
from jax.experimental import pallas as pl
from jax.experimental.pallas import tpu as pltpu
from jax.sharding import PartitionSpec as P

QUERY_HEADS = 24
KEY_VALUE_HEADS = 8
HEAD_SIZE = 64
BF16 = jnp.bfloat16
F32 = jnp.float32
ALL = ("fsdp", "rep")
SMALL = 128
LIGHT = pl.CostEstimate(flops=1000, bytes_accessed=1000, transcendentals=0)


def rms_scale(value_rows, gain_vec):
    inverse = lax.rsqrt(jnp.mean(value_rows * value_rows, axis=-1, keepdims=True) + 1e-05)
    return value_rows * inverse * gain_vec


def rotation(expert_slot_count, head_dim):
    half_dim = head_dim // 2
    frequency = jnp.exp(
        -jnp.log(10000.0) * 2.0 * jnp.arange(half_dim, dtype=jnp.float32) / head_dim
    )
    angles = jnp.arange(expert_slot_count, dtype=jnp.float32)[:, None] * frequency[None, :]
    return (jnp.cos(angles), jnp.sin(angles))


def slot_table(choices_row, length, experts, capacity):
    slots = choices_row.shape[0]
    valid = (jnp.arange(slots, dtype=jnp.int32) < length)[:, None]
    chosen = jnp.any(
        choices_row[:, :, None] == jnp.arange(experts, dtype=jnp.int32)[None, None, :], axis=1
    )
    hit = (chosen & valid).astype(F32)
    rows = jnp.arange(slots, dtype=jnp.int32)
    earlier = (rows[None, :] < rows[:, None]).astype(BF16)
    position = jnp.dot(earlier, hit.astype(BF16), preferred_element_type=F32).astype(jnp.int32)
    kept = chosen & valid & (position < capacity)
    return jnp.where(kept, position, jnp.where(chosen, -1, -2))


def chosen_gates(logits, table):
    chosen = table >= -1
    masked = jnp.where(chosen, logits, -1e30)
    top = jnp.max(masked, axis=-1, keepdims=True)
    raised = jnp.where(chosen, jnp.exp(masked - top), 0.0)
    return raised / jnp.sum(raised, axis=-1, keepdims=True)


def ring_order(size):
    if size % 2:
        return list(range(size))
    return list(range(0, size, 2)) + list(range(size - 1, 0, -2))


def tie(values, deps):
    anywhere = pl.BlockSpec(memory_space=pl.ANY)
    return pl.pallas_call(
        lambda *refs: None,
        out_shape=[jax.ShapeDtypeStruct(v.shape, v.dtype) for v in values],
        in_specs=[anywhere] * (len(values) + len(deps)),
        out_specs=[anywhere] * len(values),
        input_output_aliases={i: i for i in range(len(values))},
        cost_estimate=LIGHT,
    )(*values, *deps)


def swap(value, axis, bit):
    size = lax.axis_size(axis)
    return lax.ppermute(value, axis, [(i, i ^ bit) for i in range(size)])


def shift(value, order, step):
    size = len(order)
    return lax.ppermute(value, "fsdp", [(order[i], order[(i + step) % size]) for i in range(size)])


def ring_start(value, order, steps):
    found = {0: value}
    for step in range(1, min(steps, (len(order) - 1) // 2) + 1):
        found[-step] = shift(found[1 - step], order, 1)
        found[step] = shift(found[step - 1], order, -1)
    return found


def ring_finish(found, order, deps):
    size = len(order)
    found = dict(found)
    reach = max(found)
    back, ahead = found[-reach], found[reach]
    if deps:
        back, ahead = tie([back, ahead], deps)
    for step in range(reach + 1, (size - 1) // 2 + 1):
        back = shift(back, order, 1)
        ahead = shift(ahead, order, -1)
        found[-step] = back
        found[step] = ahead
    if size % 2 == 0:
        half = back.shape[0] // 2
        top = shift(back[:half], order, 1)
        bottom = shift(ahead[half:], order, -1)
        found[size // 2] = jnp.concatenate([top, bottom], axis=0)
    return found


def add_low(left, right):
    return (left.astype(F32) + right.astype(F32)).astype(BF16)


def ring_scatter(parts, order):
    size = len(order)
    near = (size - 1) // 2
    if size % 2 == 0:
        far = parts[size // 2]
        half = far.shape[0] // 2
        top = shift(far[:half], order, 1)
        bottom = shift(far[half:], order, -1)
        ahead, back = parts[near], parts[-near]
        ahead = jnp.concatenate([add_low(ahead[:half], top), ahead[half:]], axis=0)
        back = jnp.concatenate([back[:half], add_low(back[half:], bottom)], axis=0)
    else:
        ahead, back = parts[near], parts[-near]
    stages = [[ahead, back]]
    for step in range(near, 0, -1):
        ahead = shift(ahead, order, 1)
        back = shift(back, order, -1)
        if step > 1:
            ahead = add_low(parts[step - 1], ahead)
            back = add_low(parts[1 - step], back)
        stages.append([ahead, back])
    return ahead, back, stages


def three_way(value):
    high = value.astype(BF16)
    rest = value - high.astype(F32)
    middle = rest.astype(BF16)
    low = (rest - middle.astype(F32)).astype(BF16)
    return high, middle, low


def dot_nn(left, right):
    return jnp.dot(left, right, preferred_element_type=F32)


def dot_nt(left, right):
    return lax.dot_general(left, right, (((1,), (1,)), ((), ())), preferred_element_type=F32)


def dot_tn(left, right):
    return lax.dot_general(left, right, (((0,), (0,)), ((), ())), preferred_element_type=F32)


def tile_rotate(value, cosine, sine_left, sine_right):
    tiles = []
    for start in range(0, value.shape[1], SMALL):
        tile = value[:, start : start + SMALL]
        ahead = pltpu.roll(tile, SMALL - HEAD_SIZE // 2, axis=1)
        behind = pltpu.roll(tile, HEAD_SIZE // 2, axis=1)
        tiles.append(tile * cosine + ahead * sine_left + behind * sine_right)
    return jnp.concatenate(tiles, axis=1)


def half_variants(tile):
    lanes = lax.broadcasted_iota(jnp.int32, tile.shape, 1)
    wide = tile.astype(F32)
    turned = pltpu.roll(wide, HEAD_SIZE, axis=1)
    pick = lambda source, half: jnp.where((lanes >= HEAD_SIZE) == (half == 1), source, 0.0).astype(BF16)
    return {(c, a): pick(wide if c == a else turned, a) for c in range(2) for a in range(2)}


def row_blocks(slots):
    size = min(256, slots)
    return [(start, size, start + size) for start in range(0, slots, size)]


def allowed_block(start, size, keys, length):
    query = start + lax.broadcasted_iota(jnp.int32, (size, keys), 0)
    key = lax.broadcasted_iota(jnp.int32, (size, keys), 1)
    return (key <= query) & (key < length)


def attention_kernel(
    length_ref, x_ref, wq_ref, wk_ref, wv_ref, cos_ref, left_ref, right_ref, *rest
):
    q_ref, k_ref, v_ref, mixed_ref, lse_ref = rest[-5:]
    x = x_ref[...]
    slots = x.shape[0]
    tables = (cos_ref[...], left_ref[...], right_ref[...])
    q = tile_rotate(dot_nn(x, wq_ref[...]), *tables).astype(BF16)
    k = tile_rotate(dot_nn(x, wk_ref[...]), *tables).astype(BF16)
    v = dot_nn(x, wv_ref[...]).astype(BF16)
    q_ref[...] = q
    k_ref[...] = k
    v_ref[...] = v
    keys, values = half_variants(k), half_variants(v)
    heads = q.shape[1] // HEAD_SIZE
    group = heads // 2
    scale = 1.0 / math.sqrt(HEAD_SIZE)
    for start, size, seen in row_blocks(slots):
        allowed = allowed_block(start, size, seen, length_ref[0])
        lanes = lax.broadcasted_iota(jnp.int32, (size, SMALL), 1)
        lse = jnp.zeros((size, SMALL), F32)
        for tile in range(heads // 2):
            q_tile = q[start : start + size, tile * SMALL : (tile + 1) * SMALL]
            total = jnp.zeros((size, SMALL), F32)
            for half in range(2):
                head = 2 * tile + half
                which = (head // group, half)
                scores = dot_nt(q_tile, keys[which][:seen]) * scale
                scores = jnp.where(allowed, scores, -1e30)
                top = jnp.max(scores, axis=1, keepdims=True)
                raised = jnp.exp(scores - top)
                mass = jnp.sum(raised, axis=1, keepdims=True)
                probs = (raised * (1.0 / mass)).astype(BF16)
                total = total + dot_nn(probs, values[which][:seen])
                lse = jnp.where(lanes == head, top + jnp.log(mass), lse)
            mixed_ref[start : start + size, tile * SMALL : (tile + 1) * SMALL] = total.astype(BF16)
        lse_ref[0, start : start + size] = lse


def attention_back_kernel(
    length_ref, ga_ref, wo_ref, q_ref, k_ref, v_ref, lse_ref, cos_ref, left_ref, right_ref, *rest
):
    gq_ref, gk_ref, gv_ref = rest[-3:]
    slots = ga_ref.shape[0]
    q, k, v = q_ref[...], k_ref[...], v_ref[...]
    grad_mixed = dot_nt(ga_ref[...], wo_ref[...]).astype(BF16)
    keys, values = half_variants(k), half_variants(v)
    heads = q.shape[1] // HEAD_SIZE
    group = heads // 2
    scale = 1.0 / math.sqrt(HEAD_SIZE)
    blocks = row_blocks(slots)
    pairs = [(c, a) for c in range(2) for a in range(2)]
    zero = lambda: [jnp.zeros((size, SMALL), F32) for _, size, _ in blocks]
    gk, gv = {p: zero() for p in pairs}, {p: zero() for p in pairs}
    turn = (cos_ref[...], -left_ref[...], -right_ref[...])
    for start, size, seen in blocks:
        allowed = allowed_block(start, size, seen, length_ref[0])
        rows = slice(start, start + size)
        for tile in range(heads // 2):
            columns = slice(tile * SMALL, (tile + 1) * SMALL)
            q_tile, g_tile = q[rows, columns], grad_mixed[rows, columns]
            total = jnp.zeros((size, SMALL), F32)
            for half in range(2):
                head = 2 * tile + half
                which = (head // group, half)
                scores = dot_nt(q_tile, keys[which][:seen]) * scale
                probs = jnp.where(allowed, jnp.exp(scores - lse_ref[0, rows, head : head + 1]), 0.0)
                grad_probs = dot_nt(g_tile, values[which][:seen])
                weighted = probs * grad_probs
                grad_scores = weighted - probs * jnp.sum(weighted, axis=1, keepdims=True)
                grad_scores = grad_scores.astype(BF16)
                probs_low = probs.astype(BF16)
                total = total + dot_nn(grad_scores, keys[which][:seen])
                gv_part = dot_tn(probs_low, g_tile)
                gk_part = dot_tn(grad_scores, q_tile)
                for b, (key_start, key_size, _) in enumerate(blocks):
                    if key_start < seen:
                        piece = slice(key_start, key_start + key_size)
                        gv[which][b] = gv[which][b] + gv_part[piece]
                        gk[which][b] = gk[which][b] + gk_part[piece]
            turned = tile_rotate(total * scale, *[t[rows] for t in turn])
            gq_ref[rows, columns] = turned.astype(BF16)

    for b, (start, size, _) in enumerate(blocks):
        rows = slice(start, start + size)
        lanes = lax.broadcasted_iota(jnp.int32, (size, SMALL), 1)
        right = lanes >= HEAD_SIZE

        def joined(parts):
            placed = []
            for c in range(2):
                kept = parts[(c, c)][b]
                moved = pltpu.roll(parts[(c, 1 - c)][b], HEAD_SIZE, axis=1)
                placed.append(kept + moved)
            return jnp.where(right, placed[1], placed[0])

        gv_ref[rows] = joined(gv).astype(BF16)
        gk_ref[rows] = tile_rotate(joined(gk) * scale, *[t[rows] for t in turn]).astype(BF16)


def rotary_tables(slots):
    cosine, sine = rotation(slots, HEAD_SIZE)
    zero = jnp.zeros_like(sine)
    tile = lambda left, right: jnp.concatenate([left, right] * (SMALL // HEAD_SIZE), axis=1)
    return tile(cosine, cosine), tile(-sine, zero), tile(zero, sine)


def head_steps(k_width):
    return k_width // SMALL


def attention(length, normed, weights, tables, q_width, k_width, deps):
    slots, width = normed.shape
    steps = head_steps(k_width)
    q_block = q_width // steps
    fixed = lambda j, n: (0, 0)
    shapes = [(slots, q_width), (slots, k_width), (slots, k_width), (slots, q_width)]
    return pl.pallas_call(
        attention_kernel,
        out_shape=[jax.ShapeDtypeStruct(s, BF16) for s in shapes]
        + [jax.ShapeDtypeStruct((steps, slots, SMALL), F32)],
        grid_spec=pltpu.PrefetchScalarGridSpec(
            num_scalar_prefetch=1,
            grid=(steps,),
            in_specs=[
                pl.BlockSpec((slots, width), fixed),
                pl.BlockSpec((width, q_block), lambda j, n: (0, j)),
                pl.BlockSpec((width, SMALL), lambda j, n: (0, q_width // SMALL + j)),
                pl.BlockSpec((width, SMALL), lambda j, n: (0, (q_width + k_width) // SMALL + j)),
                pl.BlockSpec((slots, SMALL), fixed),
                pl.BlockSpec((slots, SMALL), fixed),
                pl.BlockSpec((slots, SMALL), fixed),
            ]
            + [pl.BlockSpec(memory_space=pl.ANY)] * len(deps),
            out_specs=[
                pl.BlockSpec((slots, q_block), lambda j, n: (0, j)),
                pl.BlockSpec((slots, SMALL), lambda j, n: (0, j)),
                pl.BlockSpec((slots, SMALL), lambda j, n: (0, j)),
                pl.BlockSpec((slots, q_block), lambda j, n: (0, j)),
                pl.BlockSpec((1, slots, SMALL), lambda j, n: (j, 0, 0)),
            ],
        ),
        compiler_params=pltpu.CompilerParams(
            dimension_semantics=("arbitrary",), vmem_limit_bytes=48 * 1024 * 1024
        ),
        cost_estimate=pl.CostEstimate(flops=25 * 10**9, bytes_accessed=10**7, transcendentals=10**7),
    )(length.reshape(1), normed, weights, weights, weights, *tables, *deps)


def attention_back(length, grad_attn, w_out, q, k, v, lse, tables, deps):
    slots, width = grad_attn.shape
    q_width, k_width = q.shape[1], k.shape[1]
    steps = head_steps(k_width)
    q_block = q_width // steps
    fixed = lambda j, n: (0, 0)
    shapes = [(slots, q_width), (slots, k_width), (slots, k_width)]
    q_spec = pl.BlockSpec((slots, q_block), lambda j, n: (0, j))
    k_spec = pl.BlockSpec((slots, SMALL), lambda j, n: (0, j))
    return pl.pallas_call(
        attention_back_kernel,
        out_shape=[jax.ShapeDtypeStruct(s, BF16) for s in shapes],
        grid_spec=pltpu.PrefetchScalarGridSpec(
            num_scalar_prefetch=1,
            grid=(steps,),
            in_specs=[
                pl.BlockSpec((slots, width), fixed),
                pl.BlockSpec((q_block, width), lambda j, n: (j, 0)),
                q_spec,
                k_spec,
                k_spec,
                pl.BlockSpec((1, slots, SMALL), lambda j, n: (j, 0, 0)),
                pl.BlockSpec((slots, SMALL), fixed),
                pl.BlockSpec((slots, SMALL), fixed),
                pl.BlockSpec((slots, SMALL), fixed),
            ]
            + [pl.BlockSpec(memory_space=pl.ANY)] * len(deps),
            out_specs=[q_spec, k_spec, k_spec],
        ),
        compiler_params=pltpu.CompilerParams(
            dimension_semantics=("arbitrary",), vmem_limit_bytes=48 * 1024 * 1024
        ),
        cost_estimate=pl.CostEstimate(flops=3 * 10**10, bytes_accessed=10**7, transcendentals=10**7),
    )(length.reshape(1), grad_attn, w_out, q, k, v, lse, *tables, *deps)


def out_kernel(mixed_ref, weight_ref, input_ref, gain_ref, *rest):
    hidden_ref, normed_ref = rest[-2:]
    hidden = input_ref[...].astype(F32) + dot_nn(mixed_ref[...], weight_ref[...])
    hidden_ref[...] = hidden
    normed_ref[...] = rms_scale(hidden, gain_ref[...]).astype(BF16)


def attention_out(mixed, weights, inputs, gain, deps, rows=128):
    slots, width = inputs.shape
    q_width = mixed.shape[1]
    spec = pl.BlockSpec((rows, width), lambda i: (i, 0))
    return pl.pallas_call(
        out_kernel,
        out_shape=[
            jax.ShapeDtypeStruct((slots, width), F32),
            jax.ShapeDtypeStruct((slots, width), BF16),
        ],
        grid=(slots // rows,),
        in_specs=[
            pl.BlockSpec((rows, q_width), lambda i: (i, 0)),
            pl.BlockSpec((q_width, width), lambda i: (0, 0)),
            spec,
            pl.BlockSpec((1, width), lambda i: (0, 0)),
        ]
        + [pl.BlockSpec(memory_space=pl.ANY)] * len(deps),
        out_specs=[spec, spec],
        compiler_params=pltpu.CompilerParams(
            dimension_semantics=("arbitrary",), vmem_limit_bytes=40 * 1024 * 1024
        ),
        cost_estimate=LIGHT,
    )(mixed, weights, inputs, gain.reshape(1, width), *deps)


def joint_grad_kernel(left_a_ref, right_a_ref, left_b_ref, right_b_ref, out_ref, *, steps):
    first = pl.program_id(0) < steps

    @pl.when(first)
    def _():
        out_ref[...] = dot_tn(left_a_ref[...], right_a_ref[...]).astype(BF16)

    @pl.when(jnp.logical_not(first))
    def _():
        out_ref[...] = dot_tn(left_b_ref[...], right_b_ref[...]).astype(BF16)


def joint_grad(left_a, right_a, left_b, right_b, columns=512):
    slots, rows = left_a.shape
    steps = right_a.shape[1] // columns
    width = right_a.shape[1] + right_b.shape[1]
    whole = pl.BlockSpec((slots, rows), lambda j: (0, 0))
    return pl.pallas_call(
        functools.partial(joint_grad_kernel, steps=steps),
        out_shape=jax.ShapeDtypeStruct((rows, width), BF16),
        grid=(width // columns,),
        in_specs=[
            whole,
            pl.BlockSpec((slots, columns), lambda j: (0, jnp.minimum(j, steps - 1))),
            whole,
            pl.BlockSpec((slots, columns), lambda j: (0, jnp.maximum(j - steps, 0))),
        ],
        out_specs=pl.BlockSpec((rows, columns), lambda j: (0, j)),
        compiler_params=pltpu.CompilerParams(
            dimension_semantics=("arbitrary",), vmem_limit_bytes=48 * 1024 * 1024
        ),
        cost_estimate=LIGHT,
    )(left_a, right_a, left_b, right_b)


def expert_kernel(
    first_ref,
    seq_ref,
    tok_ref,
    cot_ref,
    row_ref,
    col_ref,
    router_ref,
    gate_ref,
    up_ref,
    down_ref,
    *rest,
    padded,
):
    (
        out_ref,
        grad_ref,
        gg_ref,
        rows_ref,
        geo_ref,
        inner_ref,
        ggp_ref,
        gup_ref,
        gates_scr,
        out_acc,
        grad_acc,
    ) = rest[-11:]
    e = pl.program_id(1)
    tok = tok_ref[0]
    cot = cot_ref[0]
    slots = tok.shape[0]
    table = col_ref[0]
    lanes = lax.broadcasted_iota(jnp.int32, table.shape, 1)

    @pl.when(e == 0)
    def _():
        gates_scr[...] = chosen_gates(dot_nn(tok, router_ref[...]), table)
        out_acc[...] = jnp.zeros_like(out_acc)
        grad_acc[...] = jnp.zeros_like(grad_acc)
        gg_ref[0] = jnp.zeros_like(gg_ref[0])

    mine = lanes == first_ref[0] + e
    gate_lane = jnp.where(mine, gates_scr[...], 0.0)
    gate_col = jnp.sum(gate_lane, axis=1, keepdims=True)
    pos_col = jnp.sum(jnp.where(mine, table.astype(F32), 0.0), axis=1, keepdims=True).astype(jnp.int32)
    pos_row = row_ref[0, 0]
    pick = (lax.broadcasted_iota(jnp.int32, (padded, slots), 0) == pos_row).astype(F32).astype(BF16)
    place = (lax.broadcasted_iota(jnp.int32, (slots, padded), 1) == pos_col).astype(F32).astype(BF16)

    rows = dot_nn(pick, tok).astype(BF16)
    cot_rows = dot_nn(pick, cot)
    high, middle, low = three_way(gate_lane)
    gate_slot = dot_nn(pick, high) + dot_nn(pick, middle) + dot_nn(pick, low)
    gate_slot = jnp.sum(gate_slot, axis=1, keepdims=True)
    rows_ref[0, 0] = rows

    gate_part = dot_nn(rows, gate_ref[0])
    up_part = dot_nn(rows, up_ref[0])
    sig = 1.0 / (1.0 + jnp.exp(-gate_part))
    silu = gate_part * sig
    inner = (silu * up_part).astype(BF16)
    inner_ref[0, 0] = inner
    expert_out = dot_nn(inner, down_ref[0]).astype(BF16)
    out_acc[...] += gate_col * dot_nn(place, expert_out)

    dots = jnp.sum(cot_rows * expert_out.astype(F32), axis=1, keepdims=True)
    spread = jnp.where(lax.broadcasted_iota(jnp.int32, (padded, SMALL), 1) == e, dots, 0.0)
    high, middle, low = three_way(spread)
    gg_ref[0] += dot_nn(place, high) + dot_nn(place, middle) + dot_nn(place, low)

    geo = (gate_slot * cot_rows).astype(BF16)
    geo_ref[0, 0] = geo
    grad_inner = dot_nt(geo, down_ref[0])
    ggp = (grad_inner * up_part * sig * (1.0 + gate_part * (1.0 - sig))).astype(BF16)
    gup = (grad_inner * silu).astype(BF16)
    ggp_ref[0, 0] = ggp
    gup_ref[0, 0] = gup
    grad_rows = (dot_nt(ggp, gate_ref[0]) + dot_nt(gup, up_ref[0])).astype(BF16)
    grad_acc[...] += dot_nn(place, grad_rows)

    @pl.when(e == pl.num_programs(1) - 1)
    def _():
        out_ref[0] = out_acc[...].astype(BF16)
        grad_ref[0] = grad_acc[...].astype(BF16)


def run_experts(first, seqs, tok, cot, rows_table, cols_table, router, w_gate, w_up, w_down, padded, kept, start, total):
    count, slots, width = tok.shape
    local, _, ff = w_gate.shape
    row_block = lambda s, e, first, seq: (seq[s], first[0] + e, 0, 0)
    col_block = lambda s, e, first, seq: (seq[s], 0, 0)
    seq_block = lambda s, e, first, seq: (s, 0, 0)
    slot_block = lambda s, e, first, seq: (start + s, e, 0, 0)
    expert_block = lambda s, e, first, seq: (e, 0, 0)
    wide = jax.ShapeDtypeStruct((total, local, padded, width), BF16)
    thin = jax.ShapeDtypeStruct((total, local, padded, ff), BF16)
    whole = jax.ShapeDtypeStruct((count, slots, width), BF16)
    flops = 2 * count * local * (padded * width * (6 * ff + 4 * slots))
    moved = 4 * count * slots * width * 2 + count * local * (3 * width * ff + padded * (2 * width + 3 * ff)) * 2
    return pl.pallas_call(
        functools.partial(expert_kernel, padded=padded),
        out_shape=(
            whole,
            whole,
            jax.ShapeDtypeStruct((count, slots, SMALL), F32),
            wide,
            wide,
            thin,
            thin,
            thin,
        ),
        grid_spec=pltpu.PrefetchScalarGridSpec(
            num_scalar_prefetch=2,
            grid=(count, local),
            in_specs=[
                pl.BlockSpec((1, slots, width), seq_block),
                pl.BlockSpec((1, slots, width), seq_block),
                pl.BlockSpec((1, 1, 1, slots), row_block),
                pl.BlockSpec((1, slots, SMALL), col_block),
                pl.BlockSpec((width, SMALL), lambda s, e, first, seq: (0, 0)),
                pl.BlockSpec((1, width, ff), expert_block),
                pl.BlockSpec((1, width, ff), expert_block),
                pl.BlockSpec((1, ff, width), expert_block),
            ]
            + [pl.BlockSpec(memory_space=pl.ANY)] * len(kept),
            out_specs=[
                pl.BlockSpec((1, slots, width), seq_block),
                pl.BlockSpec((1, slots, width), seq_block),
                pl.BlockSpec((1, slots, SMALL), seq_block),
                pl.BlockSpec((1, 1, padded, width), slot_block),
                pl.BlockSpec((1, 1, padded, width), slot_block),
                pl.BlockSpec((1, 1, padded, ff), slot_block),
                pl.BlockSpec((1, 1, padded, ff), slot_block),
                pl.BlockSpec((1, 1, padded, ff), slot_block),
            ],
            scratch_shapes=[
                pltpu.VMEM((slots, SMALL), F32),
                pltpu.VMEM((slots, width), F32),
                pltpu.VMEM((slots, width), F32),
            ],
        ),
        input_output_aliases={10 + i: 3 + i for i in range(len(kept))},
        compiler_params=pltpu.CompilerParams(
            dimension_semantics=("arbitrary", "arbitrary"), vmem_limit_bytes=58 * 1024 * 1024
        ),
        cost_estimate=pl.CostEstimate(flops=flops, bytes_accessed=moved, transcendentals=count * local * padded * ff),
    )(first, seqs, tok, cot, rows_table, cols_table, router, w_gate, w_up, w_down, *kept)


def body(
    inputs,
    cotangent,
    lengths,
    choices,
    gain_attn,
    gain_moe,
    query_weight,
    key_weight,
    value_weight,
    w_out,
    w_router,
    w_gate,
    w_up,
    w_down,
):
    groups = lax.axis_size("fsdp")
    replicas = lax.axis_size("rep")
    me = lax.axis_index("fsdp")
    rep = lax.axis_index("rep")
    tokens = inputs[0].astype(F32)
    slots, width = tokens.shape
    length = lengths[0]
    choices_row = choices[0]
    top_count = choices_row.shape[1]
    local = w_gate.shape[0]
    experts = local * groups
    capacity = 25 * slots * top_count // (32 * experts)
    padded = -(-capacity // 16) * 16
    q_width = query_weight.shape[1]
    k_width = key_weight.shape[1]
    tables = rotary_tables(slots)
    order = ring_order(groups)
    place_of = [order.index(j) for j in range(groups)]
    my_place = jnp.asarray(place_of, jnp.int32)[me]

    small = jnp.concatenate(
        [
            w_router,
            gain_attn[:, None],
            gain_moe[:, None],
            jnp.zeros((w_router.shape[0], SMALL - experts - 2), BF16),
        ],
        axis=1,
    )
    share = query_weight.shape[0] // replicas

    def gather_weight(shard):
        piece = lax.dynamic_slice_in_dim(shard, rep * share, share, axis=0)
        return lax.all_gather(piece, ALL, axis=0, tiled=True)

    first_set = gather_weight(
        jnp.concatenate([query_weight, key_weight, value_weight, small], axis=1)
    )
    full_qkv = first_set[:, : q_width + 2 * k_width]
    full_small = first_set[:, q_width + 2 * k_width :]
    full_out = gather_weight(w_out)
    full_gain_attn = full_small[:, experts].astype(F32)
    full_gain_moe = full_small[:, experts + 1].astype(F32)
    lane = jnp.arange(SMALL)[None, :]
    full_router = jnp.where(lane < experts, full_small, jnp.zeros_like(full_small))

    table = slot_table(choices_row, length, experts, capacity)
    row_tables = table.T[None]
    bit = 1
    while bit < groups:
        other = swap(row_tables, "fsdp", bit)
        upper = jnp.bitwise_and(me // bit, 1) == 1
        row_tables = jnp.where(
            upper, jnp.concatenate([other, row_tables]), jnp.concatenate([row_tables, other])
        )
        bit *= 2
    col_tables = jnp.pad(
        jnp.swapaxes(row_tables, 1, 2), ((0, 0), (0, 0), (0, SMALL - experts)), constant_values=-2
    )
    row_tables = row_tables[:, :, None, :]
    cot_ring = ring_start(tie([cotangent[0]], [row_tables])[0], order, 2)

    normed_float, norm_one_pull = jax.vjp(rms_scale, tokens, full_gain_attn)
    attention_normed = normed_float.astype(BF16)
    rot_queries, rot_keys, value_rows, mixed, log_total = attention(
        length, attention_normed, first_set, tables, q_width, k_width, [row_tables, col_tables]
    )
    rows_index = jnp.arange(slots, dtype=jnp.int32)
    near_cot = [cot_ring[o] for o in (1, -1, 2, -2) if o in cot_ring]
    cot_ring = ring_finish(cot_ring, order, [mixed])
    hidden, normed_two = attention_out(
        mixed, full_out, inputs[0], full_gain_moe, near_cot
    )
    norm_two_pull = jax.vjp(rms_scale, hidden, full_gain_moe)[1]

    tok_ring = ring_finish(ring_start(normed_two, order, 1), order, [])
    gates = chosen_gates(
        jnp.dot(normed_two, full_router, preferred_element_type=F32)[:, :experts], table
    )
    valid_rows = (rows_index < length)[:, None]
    grad_y = jnp.where(valid_rows, cotangent[0].astype(F32), 0.0)

    near = (groups - 1) // 2
    arrivals = [(0,)] + [(-s, s) for s in range(1, near + 1)]
    if groups % 2 == 0:
        arrivals.append((groups // 2,))
    order_array = jnp.asarray(order, jnp.int32)
    first = (me * local).astype(jnp.int32).reshape(1)
    out_parts, grad_parts, gate_dots, kept, start = {}, {}, {}, (), 0
    for offsets in arrivals:
        seqs = order_array[(my_place + jnp.asarray(offsets, jnp.int32)) % groups]
        tok = jnp.stack([tok_ring[s] for s in offsets])
        cot = jnp.stack([cot_ring[s] for s in offsets])
        part_out, part_grad, dots, *kept = run_experts(
            first, seqs, tok, cot, row_tables, col_tables, full_router, w_gate, w_up, w_down,
            padded, kept, start, groups,
        )
        for j, s in enumerate(offsets):
            out_parts[s] = part_out[j]
            grad_parts[s] = part_grad[j]
            gate_dots[s % groups] = dots[j, :, :local].T
        start += len(offsets)
    rows_all, geo_all, inner_all, ggp_all, gup_all = kept

    by_offset = jnp.stack([gate_dots[s] for s in range(groups)])
    natural = by_offset[(jnp.asarray(place_of, jnp.int32) - my_place) % groups]
    grad_gates = lax.all_to_all(natural, "fsdp", split_axis=0, concat_axis=0, tiled=True)
    grad_gates = grad_gates.reshape(experts, slots).T

    grad_down = jnp.einsum("necf,necd->efd", inner_all, geo_all, preferred_element_type=F32)
    grad_gate = jnp.einsum("necd,necf->edf", rows_all, ggp_all, preferred_element_type=F32)
    grad_up = jnp.einsum("necd,necf->edf", rows_all, gup_all, preferred_element_type=F32)
    core_bit = jnp.bitwise_and(rep, 1)
    expert_sums = []
    for grad in (grad_gate, grad_up, grad_down):
        pairs = grad.astype(BF16).reshape(local // 2, 2, *grad.shape[1:])
        mine = lax.dynamic_index_in_dim(pairs, core_bit, 1, keepdims=False)
        other = lax.dynamic_index_in_dim(pairs, 1 - core_bit, 1, keepdims=False)
        expert_sums.append(add_low(mine, swap(other, "rep", 1)))

    left, right, _ = ring_scatter(grad_parts, order)
    (own_grads,) = tie([grad_parts[0]], expert_sums)
    grad_normed_two = own_grads.astype(F32) + left.astype(F32) + right.astype(F32)

    grad_logits = gates * (grad_gates - jnp.sum(gates * grad_gates, axis=-1, keepdims=True))
    grad_logits = grad_logits.astype(BF16)
    grad_normed_two = grad_normed_two + jnp.einsum(
        "se,de->sd", grad_logits, full_router[:, :experts], preferred_element_type=F32
    )
    grad_router = jnp.einsum("sd,se->ed", normed_two, grad_logits, preferred_element_type=F32)
    grad_hidden_norm, grad_gain_moe = norm_two_pull(grad_normed_two)
    grad_hidden = grad_y + grad_hidden_norm
    grad_attn = grad_hidden.astype(BF16)

    def reduce_weight(grad):
        owned = lax.psum_scatter(grad.astype(BF16), ALL, scatter_dimension=0, tiled=True)
        return [lax.all_gather(p, "rep", axis=0, tiled=True) for p in jnp.split(owned, 2, axis=1)]

    keys = sorted(out_parts)
    held = dict(zip(keys, tie([out_parts[o] for o in keys], [grad_attn])))
    out_left, out_right, stages = ring_scatter(held, order)
    mixture = held[0].astype(F32) + out_left.astype(F32) + out_right.astype(F32)
    output = jnp.where(valid_rows, hidden + mixture, 0.0).astype(BF16)

    grad_queries, grad_keys, grad_values = attention_back(
        length, grad_attn, full_out, rot_queries, rot_keys, value_rows, log_total, tables, []
    )
    projected = jnp.concatenate([grad_queries, grad_keys, grad_values], axis=1)
    crossed = [add_low(expert_sums[0], swap(expert_sums[0], "rep", 2))]
    (projected,) = tie([projected], [*stages[0], *crossed])
    grad_qkv = joint_grad(attention_normed, projected, mixed, grad_attn)
    (projected,) = tie([projected], [grad_qkv, *stages[min(1, len(stages) - 1)]])
    grad_normed_one = jnp.einsum("sa,da->sd", projected, full_qkv, preferred_element_type=F32)
    grad_tokens_norm, grad_gain_attn = norm_one_pull(grad_normed_one)
    grad_input = (grad_hidden + grad_tokens_norm).astype(BF16)
    total_first = jnp.concatenate(reduce_weight(grad_qkv), axis=1).astype(F32)
    small_sum = jnp.concatenate([grad_router, grad_gain_attn[None], grad_gain_moe[None]], axis=0)
    (small_sum,) = tie([small_sum.astype(BF16)], stages[min(2, len(stages) - 1)])
    for axis, size in (("fsdp", groups), ("rep", replicas)):
        bit = 1
        while bit < size:
            small_sum = add_low(small_sum, swap(small_sum, axis, bit))
            bit *= 2
    small_sum = small_sum.astype(F32)
    small_sum = lax.dynamic_slice_in_dim(small_sum, me * gain_attn.shape[0], gain_attn.shape[0], axis=1)

    later_sums = tie(expert_sums[1:], stages[min(2, len(stages) - 1)])
    expert_grads = []
    for total in (*crossed, *[add_low(t, swap(t, "rep", 2)) for t in later_sums]):
        bit = 4
        while bit < replicas:
            total = add_low(total, swap(total, "rep", bit))
            bit *= 2
        other = swap(total, "rep", 1)
        pair = jnp.where(core_bit == 0, jnp.stack([total, other], 1), jnp.stack([other, total], 1))
        expert_grads.append(pair.reshape(local, *total.shape[1:]).astype(F32))
    return (
        output[None],
        grad_input[None],
        small_sum[experts],
        small_sum[experts + 1],
        total_first[:, :q_width],
        total_first[:, q_width : q_width + k_width],
        total_first[:, q_width + k_width : q_width + 2 * k_width],
        total_first[:, q_width + 2 * k_width :],
        small_sum[:experts].T,
        *expert_grads,
    )


def solution(mesh):
    in_specs = (
        P(("rep", "fsdp"), None, None),
        P(("rep", "fsdp"), None, None),
        P(("rep", "fsdp")),
        P(("rep", "fsdp"), None, None),
        P("fsdp"),
        P("fsdp"),
        P("fsdp", None),
        P("fsdp", None),
        P("fsdp", None),
        P("fsdp", None),
        P("fsdp", None),
        P("fsdp", None, None),
        P("fsdp", None, None),
        P("fsdp", None, None),
    )
    out_specs = (
        P(("rep", "fsdp"), None, None),
        P(("rep", "fsdp"), None, None),
        P("fsdp"),
        P("fsdp"),
        P("fsdp", None),
        P("fsdp", None),
        P("fsdp", None),
        P("fsdp", None),
        P("fsdp", None),
        P("fsdp", None, None),
        P("fsdp", None, None),
        P("fsdp", None, None),
    )
    return jax.shard_map(body, mesh=mesh, in_specs=in_specs, out_specs=out_specs, check_vma=False)
```

```python
import functools
import math

import jax
import jax.numpy as jnp
from jax import lax
from jax.experimental import pallas as pl
from jax.experimental.pallas import tpu as pltpu
from jax.sharding import PartitionSpec as P

QUERY_HEADS = 24
KEY_VALUE_HEADS = 8
HEAD_SIZE = 64
BF16 = jnp.bfloat16
F32 = jnp.float32
ALL = ("fsdp", "rep")
SMALL = 128
LIGHT = pl.CostEstimate(flops=1000, bytes_accessed=1000, transcendentals=0)


def rms_scale(value_rows, gain_vec):
    inverse = lax.rsqrt(jnp.mean(value_rows * value_rows, axis=-1, keepdims=True) + 1e-05)
    return value_rows * inverse * gain_vec


def rotation(expert_slot_count, head_dim):
    half_dim = head_dim // 2
    frequency = jnp.exp(
        -jnp.log(10000.0) * 2.0 * jnp.arange(half_dim, dtype=jnp.float32) / head_dim
    )
    angles = jnp.arange(expert_slot_count, dtype=jnp.float32)[:, None] * frequency[None, :]
    return (jnp.cos(angles), jnp.sin(angles))


def slot_table(choices_row, length, experts, capacity):
    slots = choices_row.shape[0]
    valid = (jnp.arange(slots, dtype=jnp.int32) < length)[:, None]
    chosen = jnp.any(
        choices_row[:, :, None] == jnp.arange(experts, dtype=jnp.int32)[None, None, :], axis=1
    )
    hit = (chosen & valid).astype(F32)
    rows = jnp.arange(slots, dtype=jnp.int32)
    earlier = (rows[None, :] < rows[:, None]).astype(BF16)
    position = jnp.dot(earlier, hit.astype(BF16), preferred_element_type=F32).astype(jnp.int32)
    kept = chosen & valid & (position < capacity)
    return jnp.where(kept, position, jnp.where(chosen, -1, -2))


def chosen_gates(logits, table):
    chosen = table >= -1
    masked = jnp.where(chosen, logits, -1e30)
    top = jnp.max(masked, axis=-1, keepdims=True)
    raised = jnp.where(chosen, jnp.exp(masked - top), 0.0)
    return raised / jnp.sum(raised, axis=-1, keepdims=True)


def ring_order(size):
    if size % 2:
        return list(range(size))
    return list(range(0, size, 2)) + list(range(size - 1, 0, -2))


def tie(values, deps):
    anywhere = pl.BlockSpec(memory_space=pl.ANY)
    return pl.pallas_call(
        lambda *refs: None,
        out_shape=[jax.ShapeDtypeStruct(v.shape, v.dtype) for v in values],
        in_specs=[anywhere] * (len(values) + len(deps)),
        out_specs=[anywhere] * len(values),
        input_output_aliases={i: i for i in range(len(values))},
        cost_estimate=LIGHT,
    )(*values, *deps)


def swap(value, axis, bit):
    size = lax.axis_size(axis)
    return lax.ppermute(value, axis, [(i, i ^ bit) for i in range(size)])


def shift(value, order, step):
    size = len(order)
    return lax.ppermute(value, "fsdp", [(order[i], order[(i + step) % size]) for i in range(size)])


def ring_start(value, order, steps):
    found = {0: value}
    for step in range(1, min(steps, (len(order) - 1) // 2) + 1):
        found[-step] = shift(found[1 - step], order, 1)
        found[step] = shift(found[step - 1], order, -1)
    return found


def ring_finish(found, order, deps):
    size = len(order)
    found = dict(found)
    reach = max(found)
    back, ahead = found[-reach], found[reach]
    if deps:
        back, ahead = tie([back, ahead], deps)
    for step in range(reach + 1, (size - 1) // 2 + 1):
        back = shift(back, order, 1)
        ahead = shift(ahead, order, -1)
        found[-step] = back
        found[step] = ahead
    if size % 2 == 0:
        half = back.shape[0] // 2
        top = shift(back[:half], order, 1)
        bottom = shift(ahead[half:], order, -1)
        found[size // 2] = jnp.concatenate([top, bottom], axis=0)
    return found


def add_low(left, right):
    return (left.astype(F32) + right.astype(F32)).astype(BF16)


def ring_scatter(parts, order):
    size = len(order)
    near = (size - 1) // 2
    if size % 2 == 0:
        far = parts[size // 2]
        half = far.shape[0] // 2
        top = shift(far[:half], order, 1)
        bottom = shift(far[half:], order, -1)
        first = [top, bottom]
        ahead, back = parts[near], parts[-near]
        ahead = jnp.concatenate([add_low(ahead[:half], top), ahead[half:]], axis=0)
        back = jnp.concatenate([back[:half], add_low(back[half:], bottom)], axis=0)
    else:
        ahead, back = parts[near], parts[-near]
        first = []
    stages = [[ahead, back]]
    for step in range(near, 0, -1):
        ahead = shift(ahead, order, 1)
        back = shift(back, order, -1)
        if step > 1:
            ahead = add_low(parts[step - 1], ahead)
            back = add_low(parts[1 - step], back)
        stages.append([ahead, back])
    return ahead, back, stages, first


def three_way(value):
    high = value.astype(BF16)
    rest = value - high.astype(F32)
    middle = rest.astype(BF16)
    low = (rest - middle.astype(F32)).astype(BF16)
    return high, middle, low


def dot_nn(left, right):
    return jnp.dot(left, right, preferred_element_type=F32)


def dot_nt(left, right):
    return lax.dot_general(left, right, (((1,), (1,)), ((), ())), preferred_element_type=F32)


def dot_tn(left, right):
    return lax.dot_general(left, right, (((0,), (0,)), ((), ())), preferred_element_type=F32)


def tile_rotate(value, cosine, sine_left, sine_right):
    tiles = []
    for start in range(0, value.shape[1], SMALL):
        tile = value[:, start : start + SMALL]
        ahead = pltpu.roll(tile, SMALL - HEAD_SIZE // 2, axis=1)
        behind = pltpu.roll(tile, HEAD_SIZE // 2, axis=1)
        tiles.append(tile * cosine + ahead * sine_left + behind * sine_right)
    return jnp.concatenate(tiles, axis=1)


def half_variants(tile):
    lanes = lax.broadcasted_iota(jnp.int32, tile.shape, 1)
    wide = tile.astype(F32)
    turned = pltpu.roll(wide, HEAD_SIZE, axis=1)
    pick = lambda source, half: jnp.where((lanes >= HEAD_SIZE) == (half == 1), source, 0.0).astype(BF16)
    return {(c, a): pick(wide if c == a else turned, a) for c in range(2) for a in range(2)}


def row_blocks(slots):
    size = min(256, slots)
    return [(start, size, start + size) for start in range(0, slots, size)]


def allowed_block(start, size, keys, length):
    query = start + lax.broadcasted_iota(jnp.int32, (size, keys), 0)
    key = lax.broadcasted_iota(jnp.int32, (size, keys), 1)
    return (key <= query) & (key < length)


def attention_kernel(
    length_ref, x_ref, wq_ref, wk_ref, wv_ref, cos_ref, left_ref, right_ref, *rest
):
    q_ref, k_ref, v_ref, mixed_ref, lse_ref = rest[-5:]
    x = x_ref[...]
    slots = x.shape[0]
    tables = (cos_ref[...], left_ref[...], right_ref[...])
    q = tile_rotate(dot_nn(x, wq_ref[...]), *tables).astype(BF16)
    k = tile_rotate(dot_nn(x, wk_ref[...]), *tables).astype(BF16)
    v = dot_nn(x, wv_ref[...]).astype(BF16)
    q_ref[...] = q
    k_ref[...] = k
    v_ref[...] = v
    keys, values = half_variants(k), half_variants(v)
    heads = q.shape[1] // HEAD_SIZE
    group = heads // 2
    scale = 1.0 / math.sqrt(HEAD_SIZE)
    for start, size, seen in row_blocks(slots):
        allowed = allowed_block(start, size, seen, length_ref[0])
        lanes = lax.broadcasted_iota(jnp.int32, (size, SMALL), 1)
        lse = jnp.zeros((size, SMALL), F32)
        for tile in range(heads // 2):
            q_tile = q[start : start + size, tile * SMALL : (tile + 1) * SMALL]
            total = jnp.zeros((size, SMALL), F32)
            for half in range(2):
                head = 2 * tile + half
                which = (head // group, half)
                scores = dot_nt(q_tile, keys[which][:seen]) * scale
                scores = jnp.where(allowed, scores, -1e30)
                top = jnp.max(scores, axis=1, keepdims=True)
                raised = jnp.exp(scores - top)
                mass = jnp.sum(raised, axis=1, keepdims=True)
                probs = (raised * (1.0 / mass)).astype(BF16)
                total = total + dot_nn(probs, values[which][:seen])
                lse = jnp.where(lanes == head, top + jnp.log(mass), lse)
            mixed_ref[start : start + size, tile * SMALL : (tile + 1) * SMALL] = total.astype(BF16)
        lse_ref[0, start : start + size] = lse


def attention_back_kernel(
    length_ref, ga_ref, wo_ref, q_ref, k_ref, v_ref, lse_ref, cos_ref, left_ref, right_ref, *rest
):
    gq_ref, gk_ref, gv_ref = rest[-3:]
    slots = ga_ref.shape[0]
    q, k, v = q_ref[...], k_ref[...], v_ref[...]
    grad_mixed = dot_nt(ga_ref[...], wo_ref[...]).astype(BF16)
    keys, values = half_variants(k), half_variants(v)
    heads = q.shape[1] // HEAD_SIZE
    group = heads // 2
    scale = 1.0 / math.sqrt(HEAD_SIZE)
    blocks = row_blocks(slots)
    pairs = [(c, a) for c in range(2) for a in range(2)]
    zero = lambda: [jnp.zeros((size, SMALL), F32) for _, size, _ in blocks]
    gk, gv = {p: zero() for p in pairs}, {p: zero() for p in pairs}
    turn = (cos_ref[...], -left_ref[...], -right_ref[...])
    for start, size, seen in blocks:
        allowed = allowed_block(start, size, seen, length_ref[0])
        rows = slice(start, start + size)
        for tile in range(heads // 2):
            columns = slice(tile * SMALL, (tile + 1) * SMALL)
            q_tile, g_tile = q[rows, columns], grad_mixed[rows, columns]
            total = jnp.zeros((size, SMALL), F32)
            for half in range(2):
                head = 2 * tile + half
                which = (head // group, half)
                scores = dot_nt(q_tile, keys[which][:seen]) * scale
                probs = jnp.where(allowed, jnp.exp(scores - lse_ref[0, rows, head : head + 1]), 0.0)
                grad_probs = dot_nt(g_tile, values[which][:seen])
                weighted = probs * grad_probs
                grad_scores = weighted - probs * jnp.sum(weighted, axis=1, keepdims=True)
                grad_scores = grad_scores.astype(BF16)
                probs_low = probs.astype(BF16)
                total = total + dot_nn(grad_scores, keys[which][:seen])
                gv_part = dot_tn(probs_low, g_tile)
                gk_part = dot_tn(grad_scores, q_tile)
                for b, (key_start, key_size, _) in enumerate(blocks):
                    if key_start < seen:
                        piece = slice(key_start, key_start + key_size)
                        gv[which][b] = gv[which][b] + gv_part[piece]
                        gk[which][b] = gk[which][b] + gk_part[piece]
            turned = tile_rotate(total * scale, *[t[rows] for t in turn])
            gq_ref[rows, columns] = turned.astype(BF16)

    for b, (start, size, _) in enumerate(blocks):
        rows = slice(start, start + size)
        lanes = lax.broadcasted_iota(jnp.int32, (size, SMALL), 1)
        right = lanes >= HEAD_SIZE

        def joined(parts):
            placed = []
            for c in range(2):
                kept = parts[(c, c)][b]
                moved = pltpu.roll(parts[(c, 1 - c)][b], HEAD_SIZE, axis=1)
                placed.append(kept + moved)
            return jnp.where(right, placed[1], placed[0])

        gv_ref[rows] = joined(gv).astype(BF16)
        gk_ref[rows] = tile_rotate(joined(gk) * scale, *[t[rows] for t in turn]).astype(BF16)


def rotary_tables(slots):
    cosine, sine = rotation(slots, HEAD_SIZE)
    zero = jnp.zeros_like(sine)
    tile = lambda left, right: jnp.concatenate([left, right] * (SMALL // HEAD_SIZE), axis=1)
    return tile(cosine, cosine), tile(-sine, zero), tile(zero, sine)


def head_steps(k_width):
    return k_width // SMALL


def attention(length, normed, weights, tables, q_width, k_width, deps):
    slots, width = normed.shape
    steps = head_steps(k_width)
    q_block = q_width // steps
    fixed = lambda j, n: (0, 0)
    shapes = [(slots, q_width), (slots, k_width), (slots, k_width), (slots, q_width)]
    return pl.pallas_call(
        attention_kernel,
        out_shape=[jax.ShapeDtypeStruct(s, BF16) for s in shapes]
        + [jax.ShapeDtypeStruct((steps, slots, SMALL), F32)],
        grid_spec=pltpu.PrefetchScalarGridSpec(
            num_scalar_prefetch=1,
            grid=(steps,),
            in_specs=[
                pl.BlockSpec((slots, width), fixed),
                pl.BlockSpec((width, q_block), lambda j, n: (0, j)),
                pl.BlockSpec((width, SMALL), lambda j, n: (0, q_width // SMALL + j)),
                pl.BlockSpec((width, SMALL), lambda j, n: (0, (q_width + k_width) // SMALL + j)),
                pl.BlockSpec((slots, SMALL), fixed),
                pl.BlockSpec((slots, SMALL), fixed),
                pl.BlockSpec((slots, SMALL), fixed),
            ]
            + [pl.BlockSpec(memory_space=pl.ANY)] * len(deps),
            out_specs=[
                pl.BlockSpec((slots, q_block), lambda j, n: (0, j)),
                pl.BlockSpec((slots, SMALL), lambda j, n: (0, j)),
                pl.BlockSpec((slots, SMALL), lambda j, n: (0, j)),
                pl.BlockSpec((slots, q_block), lambda j, n: (0, j)),
                pl.BlockSpec((1, slots, SMALL), lambda j, n: (j, 0, 0)),
            ],
        ),
        compiler_params=pltpu.CompilerParams(
            dimension_semantics=("arbitrary",), vmem_limit_bytes=48 * 1024 * 1024
        ),
        cost_estimate=pl.CostEstimate(flops=25 * 10**9, bytes_accessed=10**7, transcendentals=10**7),
    )(length.reshape(1), normed, weights, weights, weights, *tables, *deps)


def attention_back(length, grad_attn, w_out, q, k, v, lse, tables, deps):
    slots, width = grad_attn.shape
    q_width, k_width = q.shape[1], k.shape[1]
    steps = head_steps(k_width)
    q_block = q_width // steps
    fixed = lambda j, n: (0, 0)
    shapes = [(slots, q_width), (slots, k_width), (slots, k_width)]
    q_spec = pl.BlockSpec((slots, q_block), lambda j, n: (0, j))
    k_spec = pl.BlockSpec((slots, SMALL), lambda j, n: (0, j))
    return pl.pallas_call(
        attention_back_kernel,
        out_shape=[jax.ShapeDtypeStruct(s, BF16) for s in shapes],
        grid_spec=pltpu.PrefetchScalarGridSpec(
            num_scalar_prefetch=1,
            grid=(steps,),
            in_specs=[
                pl.BlockSpec((slots, width), fixed),
                pl.BlockSpec((q_block, width), lambda j, n: (j, 0)),
                q_spec,
                k_spec,
                k_spec,
                pl.BlockSpec((1, slots, SMALL), lambda j, n: (j, 0, 0)),
                pl.BlockSpec((slots, SMALL), fixed),
                pl.BlockSpec((slots, SMALL), fixed),
                pl.BlockSpec((slots, SMALL), fixed),
            ]
            + [pl.BlockSpec(memory_space=pl.ANY)] * len(deps),
            out_specs=[q_spec, k_spec, k_spec],
        ),
        compiler_params=pltpu.CompilerParams(
            dimension_semantics=("arbitrary",), vmem_limit_bytes=48 * 1024 * 1024
        ),
        cost_estimate=pl.CostEstimate(flops=3 * 10**10, bytes_accessed=10**7, transcendentals=10**7),
    )(length.reshape(1), grad_attn, w_out, q, k, v, lse, *tables, *deps)


def out_kernel(mixed_ref, weight_ref, input_ref, gain_ref, *rest):
    hidden_ref, normed_ref = rest[-2:]
    hidden = input_ref[...].astype(F32) + dot_nn(mixed_ref[...], weight_ref[...])
    hidden_ref[...] = hidden
    normed_ref[...] = rms_scale(hidden, gain_ref[...]).astype(BF16)


def attention_out(mixed, weights, inputs, gain, deps, rows=128):
    slots, width = inputs.shape
    q_width = mixed.shape[1]
    spec = pl.BlockSpec((rows, width), lambda i: (i, 0))
    return pl.pallas_call(
        out_kernel,
        out_shape=[
            jax.ShapeDtypeStruct((slots, width), F32),
            jax.ShapeDtypeStruct((slots, width), BF16),
        ],
        grid=(slots // rows,),
        in_specs=[
            pl.BlockSpec((rows, q_width), lambda i: (i, 0)),
            pl.BlockSpec((q_width, width), lambda i: (0, 0)),
            spec,
            pl.BlockSpec((1, width), lambda i: (0, 0)),
        ]
        + [pl.BlockSpec(memory_space=pl.ANY)] * len(deps),
        out_specs=[spec, spec],
        compiler_params=pltpu.CompilerParams(
            dimension_semantics=("arbitrary",), vmem_limit_bytes=40 * 1024 * 1024
        ),
        cost_estimate=LIGHT,
    )(mixed, weights, inputs, gain.reshape(1, width), *deps)


def joint_grad_kernel(left_a_ref, right_a_ref, left_b_ref, right_b_ref, out_ref, *, steps):
    first = pl.program_id(0) < steps

    @pl.when(first)
    def _():
        out_ref[...] = dot_tn(left_a_ref[...], right_a_ref[...]).astype(BF16)

    @pl.when(jnp.logical_not(first))
    def _():
        out_ref[...] = dot_tn(left_b_ref[...], right_b_ref[...]).astype(BF16)


def joint_grad(left_a, right_a, left_b, right_b, columns=512):
    slots, rows = left_a.shape
    steps = right_a.shape[1] // columns
    width = right_a.shape[1] + right_b.shape[1]
    whole = pl.BlockSpec((slots, rows), lambda j: (0, 0))
    return pl.pallas_call(
        functools.partial(joint_grad_kernel, steps=steps),
        out_shape=jax.ShapeDtypeStruct((rows, width), BF16),
        grid=(width // columns,),
        in_specs=[
            whole,
            pl.BlockSpec((slots, columns), lambda j: (0, jnp.minimum(j, steps - 1))),
            whole,
            pl.BlockSpec((slots, columns), lambda j: (0, jnp.maximum(j - steps, 0))),
        ],
        out_specs=pl.BlockSpec((rows, columns), lambda j: (0, j)),
        compiler_params=pltpu.CompilerParams(
            dimension_semantics=("arbitrary",), vmem_limit_bytes=48 * 1024 * 1024
        ),
        cost_estimate=LIGHT,
    )(left_a, right_a, left_b, right_b)


def expert_kernel(
    first_ref,
    seq_ref,
    tok_ref,
    cot_ref,
    row_ref,
    col_ref,
    router_ref,
    gate_ref,
    up_ref,
    down_ref,
    *rest,
    padded,
):
    (
        out_ref,
        grad_ref,
        gg_ref,
        rows_ref,
        geo_ref,
        inner_ref,
        ggp_ref,
        gup_ref,
        gates_scr,
        out_acc,
        grad_acc,
    ) = rest[-11:]
    e = pl.program_id(1)
    tok = tok_ref[0]
    cot = cot_ref[0]
    slots = tok.shape[0]
    table = col_ref[0]
    lanes = lax.broadcasted_iota(jnp.int32, table.shape, 1)

    @pl.when(e == 0)
    def _():
        gates_scr[...] = chosen_gates(dot_nn(tok, router_ref[...]), table)
        out_acc[...] = jnp.zeros_like(out_acc)
        grad_acc[...] = jnp.zeros_like(grad_acc)
        gg_ref[0] = jnp.zeros_like(gg_ref[0])

    mine = lanes == first_ref[0] + e
    gate_lane = jnp.where(mine, gates_scr[...], 0.0)
    gate_col = jnp.sum(gate_lane, axis=1, keepdims=True)
    pos_col = jnp.sum(jnp.where(mine, table.astype(F32), 0.0), axis=1, keepdims=True).astype(jnp.int32)
    pos_row = row_ref[0, 0]
    pick = (lax.broadcasted_iota(jnp.int32, (padded, slots), 0) == pos_row).astype(F32).astype(BF16)
    place = (lax.broadcasted_iota(jnp.int32, (slots, padded), 1) == pos_col).astype(F32).astype(BF16)

    rows = dot_nn(pick, tok).astype(BF16)
    cot_rows = dot_nn(pick, cot)
    high, middle, low = three_way(gate_lane)
    gate_slot = dot_nn(pick, high) + dot_nn(pick, middle) + dot_nn(pick, low)
    gate_slot = jnp.sum(gate_slot, axis=1, keepdims=True)
    rows_ref[0, 0] = rows

    gate_part = dot_nn(rows, gate_ref[0])
    up_part = dot_nn(rows, up_ref[0])
    sig = 1.0 / (1.0 + jnp.exp(-gate_part))
    silu = gate_part * sig
    inner = (silu * up_part).astype(BF16)
    inner_ref[0, 0] = inner
    expert_out = dot_nn(inner, down_ref[0]).astype(BF16)
    out_acc[...] += gate_col * dot_nn(place, expert_out)

    dots = jnp.sum(cot_rows * expert_out.astype(F32), axis=1, keepdims=True)
    spread = jnp.where(lax.broadcasted_iota(jnp.int32, (padded, SMALL), 1) == e, dots, 0.0)
    high, middle, low = three_way(spread)
    gg_ref[0] += dot_nn(place, high) + dot_nn(place, middle) + dot_nn(place, low)

    geo = (gate_slot * cot_rows).astype(BF16)
    geo_ref[0, 0] = geo
    grad_inner = dot_nt(geo, down_ref[0])
    ggp = (grad_inner * up_part * sig * (1.0 + gate_part * (1.0 - sig))).astype(BF16)
    gup = (grad_inner * silu).astype(BF16)
    ggp_ref[0, 0] = ggp
    gup_ref[0, 0] = gup
    grad_rows = (dot_nt(ggp, gate_ref[0]) + dot_nt(gup, up_ref[0])).astype(BF16)
    grad_acc[...] += dot_nn(place, grad_rows)

    @pl.when(e == pl.num_programs(1) - 1)
    def _():
        out_ref[0] = out_acc[...].astype(BF16)
        grad_ref[0] = grad_acc[...].astype(BF16)


def run_experts(first, seqs, tok, cot, rows_table, cols_table, router, w_gate, w_up, w_down, padded, kept, start, total):
    count, slots, width = tok.shape
    local, _, ff = w_gate.shape
    row_block = lambda s, e, first, seq: (seq[s], first[0] + e, 0, 0)
    col_block = lambda s, e, first, seq: (seq[s], 0, 0)
    seq_block = lambda s, e, first, seq: (s, 0, 0)
    slot_block = lambda s, e, first, seq: (start + s, e, 0, 0)
    expert_block = lambda s, e, first, seq: (e, 0, 0)
    wide = jax.ShapeDtypeStruct((total, local, padded, width), BF16)
    thin = jax.ShapeDtypeStruct((total, local, padded, ff), BF16)
    whole = jax.ShapeDtypeStruct((count, slots, width), BF16)
    flops = 2 * count * local * (padded * width * (6 * ff + 4 * slots))
    moved = 4 * count * slots * width * 2 + count * local * (3 * width * ff + padded * (2 * width + 3 * ff)) * 2
    return pl.pallas_call(
        functools.partial(expert_kernel, padded=padded),
        out_shape=(
            whole,
            whole,
            jax.ShapeDtypeStruct((count, slots, SMALL), F32),
            wide,
            wide,
            thin,
            thin,
            thin,
        ),
        grid_spec=pltpu.PrefetchScalarGridSpec(
            num_scalar_prefetch=2,
            grid=(count, local),
            in_specs=[
                pl.BlockSpec((1, slots, width), seq_block),
                pl.BlockSpec((1, slots, width), seq_block),
                pl.BlockSpec((1, 1, 1, slots), row_block),
                pl.BlockSpec((1, slots, SMALL), col_block),
                pl.BlockSpec((width, SMALL), lambda s, e, first, seq: (0, 0)),
                pl.BlockSpec((1, width, ff), expert_block),
                pl.BlockSpec((1, width, ff), expert_block),
                pl.BlockSpec((1, ff, width), expert_block),
            ]
            + [pl.BlockSpec(memory_space=pl.ANY)] * len(kept),
            out_specs=[
                pl.BlockSpec((1, slots, width), seq_block),
                pl.BlockSpec((1, slots, width), seq_block),
                pl.BlockSpec((1, slots, SMALL), seq_block),
                pl.BlockSpec((1, 1, padded, width), slot_block),
                pl.BlockSpec((1, 1, padded, width), slot_block),
                pl.BlockSpec((1, 1, padded, ff), slot_block),
                pl.BlockSpec((1, 1, padded, ff), slot_block),
                pl.BlockSpec((1, 1, padded, ff), slot_block),
            ],
            scratch_shapes=[
                pltpu.VMEM((slots, SMALL), F32),
                pltpu.VMEM((slots, width), F32),
                pltpu.VMEM((slots, width), F32),
            ],
        ),
        input_output_aliases={10 + i: 3 + i for i in range(len(kept))},
        compiler_params=pltpu.CompilerParams(
            dimension_semantics=("arbitrary", "arbitrary"), vmem_limit_bytes=58 * 1024 * 1024
        ),
        cost_estimate=pl.CostEstimate(flops=flops, bytes_accessed=moved, transcendentals=count * local * padded * ff),
    )(first, seqs, tok, cot, rows_table, cols_table, router, w_gate, w_up, w_down, *kept)


def body(
    inputs,
    cotangent,
    lengths,
    choices,
    gain_attn,
    gain_moe,
    query_weight,
    key_weight,
    value_weight,
    w_out,
    w_router,
    w_gate,
    w_up,
    w_down,
):
    groups = lax.axis_size("fsdp")
    replicas = lax.axis_size("rep")
    me = lax.axis_index("fsdp")
    rep = lax.axis_index("rep")
    tokens = inputs[0].astype(F32)
    slots, width = tokens.shape
    length = lengths[0]
    choices_row = choices[0]
    top_count = choices_row.shape[1]
    local = w_gate.shape[0]
    experts = local * groups
    capacity = 25 * slots * top_count // (32 * experts)
    padded = -(-capacity // 16) * 16
    q_width = query_weight.shape[1]
    k_width = key_weight.shape[1]
    tables = rotary_tables(slots)
    order = ring_order(groups)
    place_of = [order.index(j) for j in range(groups)]
    my_place = jnp.asarray(place_of, jnp.int32)[me]

    small = jnp.concatenate(
        [
            w_router,
            gain_attn[:, None],
            gain_moe[:, None],
            jnp.zeros((w_router.shape[0], SMALL - experts - 2), BF16),
        ],
        axis=1,
    )
    share = query_weight.shape[0] // replicas

    def gather_weight(shard):
        piece = lax.dynamic_slice_in_dim(shard, rep * share, share, axis=0)
        return lax.all_gather(piece, ALL, axis=0, tiled=True)

    first_set = gather_weight(
        jnp.concatenate([query_weight, key_weight, value_weight, small], axis=1)
    )
    full_qkv = first_set[:, : q_width + 2 * k_width]
    full_small = first_set[:, q_width + 2 * k_width :]
    full_out = gather_weight(w_out)
    full_gain_attn = full_small[:, experts].astype(F32)
    full_gain_moe = full_small[:, experts + 1].astype(F32)
    lane = jnp.arange(SMALL)[None, :]
    full_router = jnp.where(lane < experts, full_small, jnp.zeros_like(full_small))

    table = slot_table(choices_row, length, experts, capacity)
    row_tables = table.T[None]
    bit = 1
    while bit < groups:
        other = swap(row_tables, "fsdp", bit)
        upper = jnp.bitwise_and(me // bit, 1) == 1
        row_tables = jnp.where(
            upper, jnp.concatenate([other, row_tables]), jnp.concatenate([row_tables, other])
        )
        bit *= 2
    col_tables = jnp.pad(
        jnp.swapaxes(row_tables, 1, 2), ((0, 0), (0, 0), (0, SMALL - experts)), constant_values=-2
    )
    row_tables = row_tables[:, :, None, :]
    cot_ring = ring_start(tie([cotangent[0]], [row_tables])[0], order, 2)

    normed_float, norm_one_pull = jax.vjp(rms_scale, tokens, full_gain_attn)
    attention_normed = normed_float.astype(BF16)
    rot_queries, rot_keys, value_rows, mixed, log_total = attention(
        length, attention_normed, first_set, tables, q_width, k_width, [row_tables, col_tables]
    )
    rows_index = jnp.arange(slots, dtype=jnp.int32)
    near_cot = [cot_ring[o] for o in (1, -1, 2, -2) if o in cot_ring]
    cot_ring = ring_finish(cot_ring, order, [mixed])
    hidden, normed_two = attention_out(
        mixed, full_out, inputs[0], full_gain_moe, near_cot
    )
    norm_two_pull = jax.vjp(rms_scale, hidden, full_gain_moe)[1]

    tok_ring = ring_finish(ring_start(normed_two, order, 1), order, [])
    gates = chosen_gates(
        jnp.dot(normed_two, full_router, preferred_element_type=F32)[:, :experts], table
    )
    valid_rows = (rows_index < length)[:, None]
    grad_y = jnp.where(valid_rows, cotangent[0].astype(F32), 0.0)

    near = (groups - 1) // 2
    arrivals = [(0,)] + [(-s, s) for s in range(1, near + 1)]
    if groups % 2 == 0:
        arrivals.append((groups // 2,))
    order_array = jnp.asarray(order, jnp.int32)
    first = (me * local).astype(jnp.int32).reshape(1)
    out_parts, grad_parts, gate_dots, kept, start = {}, {}, {}, (), 0
    for offsets in arrivals:
        seqs = order_array[(my_place + jnp.asarray(offsets, jnp.int32)) % groups]
        tok = jnp.stack([tok_ring[s] for s in offsets])
        cot = jnp.stack([cot_ring[s] for s in offsets])
        part_out, part_grad, dots, *kept = run_experts(
            first, seqs, tok, cot, row_tables, col_tables, full_router, w_gate, w_up, w_down,
            padded, kept, start, groups,
        )
        for j, s in enumerate(offsets):
            out_parts[s] = part_out[j]
            grad_parts[s] = part_grad[j]
            gate_dots[s % groups] = dots[j, :, :local].T
        start += len(offsets)
    rows_all, geo_all, inner_all, ggp_all, gup_all = kept

    by_offset = jnp.stack([gate_dots[s] for s in range(groups)])
    natural = by_offset[(jnp.asarray(place_of, jnp.int32) - my_place) % groups]
    grad_gates = lax.all_to_all(natural, "fsdp", split_axis=0, concat_axis=0, tiled=True)
    grad_gates = grad_gates.reshape(experts, slots).T

    grad_down = jnp.einsum("necf,necd->efd", inner_all, geo_all, preferred_element_type=F32)
    grad_gate = jnp.einsum("necd,necf->edf", rows_all, ggp_all, preferred_element_type=F32)
    grad_up = jnp.einsum("necd,necf->edf", rows_all, gup_all, preferred_element_type=F32)
    core_bit = jnp.bitwise_and(rep, 1)
    expert_sums = []
    for grad in (grad_gate, grad_up, grad_down):
        pairs = grad.astype(BF16).reshape(local // 2, 2, *grad.shape[1:])
        mine = lax.dynamic_index_in_dim(pairs, core_bit, 1, keepdims=False)
        other = lax.dynamic_index_in_dim(pairs, 1 - core_bit, 1, keepdims=False)
        expert_sums.append(add_low(mine, swap(other, "rep", 1)))

    left, right, *_ = ring_scatter(grad_parts, order)
    (own_grads,) = tie([grad_parts[0]], expert_sums)
    grad_normed_two = own_grads.astype(F32) + left.astype(F32) + right.astype(F32)

    grad_logits = gates * (grad_gates - jnp.sum(gates * grad_gates, axis=-1, keepdims=True))
    grad_logits = grad_logits.astype(BF16)
    grad_normed_two = grad_normed_two + jnp.einsum(
        "se,de->sd", grad_logits, full_router[:, :experts], preferred_element_type=F32
    )
    grad_router = jnp.einsum("sd,se->ed", normed_two, grad_logits, preferred_element_type=F32)
    grad_hidden_norm, grad_gain_moe = norm_two_pull(grad_normed_two)
    grad_hidden = grad_y + grad_hidden_norm
    grad_attn = grad_hidden.astype(BF16)

    def reduce_weight(grad):
        owned = lax.psum_scatter(grad.astype(BF16), ALL, scatter_dimension=0, tiled=True)
        return [lax.all_gather(p, "rep", axis=0, tiled=True) for p in jnp.split(owned, 2, axis=1)]

    keys = sorted(out_parts)
    held = dict(zip(keys, tie([out_parts[o] for o in keys], [grad_attn])))
    out_left, out_right, stages, first_hop = ring_scatter(held, order)
    mixture = held[0].astype(F32) + out_left.astype(F32) + out_right.astype(F32)
    output = jnp.where(valid_rows, hidden + mixture, 0.0).astype(BF16)

    grad_queries, grad_keys, grad_values = attention_back(
        length, grad_attn, full_out, rot_queries, rot_keys, value_rows, log_total, tables, []
    )
    projected = jnp.concatenate([grad_queries, grad_keys, grad_values], axis=1)
    crossed = [add_low(expert_sums[0], swap(expert_sums[0], "rep", 2))]
    (projected,) = tie([projected], [*first_hop, *crossed])
    grad_qkv = joint_grad(attention_normed, projected, mixed, grad_attn)
    (projected,) = tie([projected], [grad_qkv, *stages[min(1, len(stages) - 1)]])
    grad_normed_one = jnp.einsum("sa,da->sd", projected, full_qkv, preferred_element_type=F32)
    grad_tokens_norm, grad_gain_attn = norm_one_pull(grad_normed_one)
    grad_input = (grad_hidden + grad_tokens_norm).astype(BF16)
    total_low, total_high = reduce_weight(grad_qkv)
    middle = total_low.shape[1]
    starts = (0, q_width, q_width + k_width, q_width + 2 * k_width)
    sides = [(total_low, a) if a < middle else (total_high, a - middle) for a in starts]
    sizes = (q_width, k_width, k_width, width)
    totals = [side[:, a : a + n].astype(F32) for (side, a), n in zip(sides, sizes)]
    small_sum = jnp.concatenate([grad_router, grad_gain_attn[None], grad_gain_moe[None]], axis=0)
    (small_sum,) = tie([small_sum.astype(BF16)], stages[min(2, len(stages) - 1)])
    for axis, size in (("fsdp", groups), ("rep", replicas)):
        bit = 1
        while bit < size:
            small_sum = add_low(small_sum, swap(small_sum, axis, bit))
            bit *= 2
    small_sum = small_sum.astype(F32)
    small_sum = lax.dynamic_slice_in_dim(small_sum, me * gain_attn.shape[0], gain_attn.shape[0], axis=1)

    later_sums = tie(expert_sums[1:], stages[min(2, len(stages) - 1)])
    expert_grads = []
    for total in (*crossed, *[add_low(t, swap(t, "rep", 2)) for t in later_sums]):
        bit = 4
        while bit < replicas:
            total = add_low(total, swap(total, "rep", bit))
            bit *= 2
        other = swap(total, "rep", 1)
        pair = jnp.where(core_bit == 0, jnp.stack([total, other], 1), jnp.stack([other, total], 1))
        expert_grads.append(pair.reshape(local, *total.shape[1:]).astype(F32))
    return (
        output[None],
        grad_input[None],
        small_sum[experts],
        small_sum[experts + 1],
        *totals,
        small_sum[:experts].T,
        *expert_grads,
    )


def solution(mesh):
    in_specs = (
        P(("rep", "fsdp"), None, None),
        P(("rep", "fsdp"), None, None),
        P(("rep", "fsdp")),
        P(("rep", "fsdp"), None, None),
        P("fsdp"),
        P("fsdp"),
        P("fsdp", None),
        P("fsdp", None),
        P("fsdp", None),
        P("fsdp", None),
        P("fsdp", None),
        P("fsdp", None, None),
        P("fsdp", None, None),
        P("fsdp", None, None),
    )
    out_specs = (
        P(("rep", "fsdp"), None, None),
        P(("rep", "fsdp"), None, None),
        P("fsdp"),
        P("fsdp"),
        P("fsdp", None),
        P("fsdp", None),
        P("fsdp", None),
        P("fsdp", None),
        P("fsdp", None),
        P("fsdp", None, None),
        P("fsdp", None, None),
        P("fsdp", None, None),
    )
    return jax.shard_map(body, mesh=mesh, in_specs=in_specs, out_specs=out_specs, check_vma=False)
```
